512 devices in a mesh: tile: 64 (over z_hi, x, y), plane: 8 (over z_lo, core).
Axes of the slice: x: 4, y: 4, z: 16 (z_hi: 4, z_lo: 4; z = z_hi * 4 + z_lo), core: 2. Of those that a mesh axis runs over, the one named last changes fastest.
Arguments:
- ref_feat: bfloat16 [32, 4, 16384], P(None, None, 'tile'), may hold values from -6 to 6
- src_feat: bfloat16 [4, 32, 4, 16384], P(None, 'plane', None, 'tile'), may hold values from -6 to 6
- shifts: int32 [4, 64], P(None, 'plane'), may hold values from 0 to 128, as said below
- conv_one: bfloat16 [8, 8, 3, 3, 3], replicated, may hold values from -0.4375 to 0.4375
- bias_one: float32 [8], replicated, may hold values from -0.5 to 0.5
- conv_two: bfloat16 [8, 8, 3, 3, 3], replicated, may hold values from -0.4375 to 0.4375
- bias_two: float32 [8], replicated, may hold values from -0.5 to 0.5
- view_head: float32 [8], replicated, may hold values from -2 to 2
Outputs:
- joined: bfloat16 [8, 64, 4, 16384], P(None, 'plane', None, 'tile')
The draws below stay inside these ranges and needn't reach their ends.
Inputs may be any that keep to these rules, and one draw needn't show every extreme that they name: `shifts`: for every view the shift never falls from one plane to the next; it is 0 at plane 0 and 128 at plane 64 - 1.
All inputs are finite; a program needn't handle non-finite values.
Results may differ from the reference program's by a relative error of at most 0.0053.
Values may be sent and summed in bfloat16 or wider, within the bound.
A program may use at most 64 MiB of HBM per device.

```python
import jax
import jax.numpy as jnp
from jax import lax

CHANNELS = 32
GROUPS = 8
CONV_CH = 8
VIEWS = 4
ROWS = 4
MAX_SHIFT = 128
PLANES = 64
WIDTH = 16384


def draw_shifts(key, part):
    values = jax.random.randint(key, (VIEWS, PLANES - 2), 0, MAX_SHIFT + 1).astype(jnp.int32)
    ordered = jnp.sort(values, axis=1)
    first = jnp.zeros((VIEWS, 1), jnp.int32)
    last = jnp.full((VIEWS, 1), MAX_SHIFT, jnp.int32)
    return jnp.concatenate([first, ordered, last], axis=1)


def steps_of(key, dims, shards, low, top_value):
    factor_of, own = 1.0, jax.random.fold_in(key, 6)
    for position, blocks in shards:
        draws = jnp.exp(jax.random.uniform(jax.random.fold_in(own, position), (blocks,), jnp.float32, low / len(shards), top_value / len(shards)))
        factor_of = factor_of * jnp.repeat(draws, dims[position] // blocks).reshape([-1 if axis == position else 1 for axis in range(len(dims))])
    return factor_of


def bell_draw(own_key, extent, width, most, pieces=(), kind=jnp.bfloat16):
    entries = jax.random.normal(own_key, extent, jnp.float32) * width
    if len(pieces) > 0:
        entries = steps_of(own_key, extent, pieces, -0.22, 0.18) * entries
    return jnp.clip(entries, min=-most, max=most).astype(kind)


def setup_inputs(seed: int = 0) -> dict:
    key_of = jax.random.split(jax.random.key(seed), 9)
    ref_feat = bell_draw(key_of[0], (CHANNELS, ROWS, WIDTH), 1.0, 6.0, ((2, 64),))
    src_feat = bell_draw(key_of[1], (VIEWS, CHANNELS, ROWS, WIDTH), 1.0, 6.0, ((1, 8), (3, 64)))
    shifts = draw_shifts(jax.random.fold_in(key_of[8], 71), 0)
    conv_one = bell_draw(key_of[3], (CONV_CH, GROUPS, 3, 3, 3), (27 * GROUPS) ** -0.5, 0.4375)
    bias_one = jnp.clip(jax.random.uniform(key_of[4], (CONV_CH,), jnp.float32, -0.5, 0.5), -0.5, 0.5)
    conv_two = bell_draw(key_of[5], (CONV_CH, CONV_CH, 3, 3, 3), (27 * CONV_CH) ** -0.5, 0.4375)
    bias_two = jnp.clip(jax.random.uniform(key_of[6], (CONV_CH,), jnp.float32, -0.5, 0.5), -0.5, 0.5)
    view_head = bell_draw(key_of[7], (CONV_CH,), CONV_CH ** -0.5, 2.0, (), jnp.float32)
    return {"ref_feat": ref_feat, "src_feat": src_feat, "shifts": shifts, "conv_one": conv_one, "bias_one": bias_one, "conv_two": conv_two, "bias_two": bias_two, "view_head": view_head}


def convolve(volume, kernel, offset):
    result = lax.conv_general_dilated(volume.astype(jnp.float32)[None], kernel.astype(jnp.float32), (1, 1, 1), [(1, 1), (1, 1), (1, 1)], dimension_numbers=("NCDHW", "OIDHW", "NCDHW"), precision=lax.Precision.HIGHEST)[0]
    return jax.nn.relu(result + offset[:, None, None, None])


def reference(ref_feat, src_feat, shifts, conv_one, bias_one, conv_two, bias_two, view_head):
    ref_wide = ref_feat.astype(jnp.float32)
    weighted = jnp.zeros((GROUPS, PLANES, ROWS, WIDTH), jnp.float32)
    total_weight = jnp.zeros((PLANES, ROWS, WIDTH), jnp.float32)
    for view_idx in range(VIEWS):
        padded = jnp.pad(src_feat[view_idx], ((0, 0), (0, 0), (MAX_SHIFT, 0)))

        def one_plane(offset):
            start = (MAX_SHIFT - offset).astype(jnp.int32)
            shifted = lax.dynamic_slice_in_dim(padded, start, WIDTH, 2).astype(jnp.float32)
            products = (ref_wide * shifted).reshape(GROUPS, CHANNELS // GROUPS, ROWS, WIDTH)
            return jnp.mean(products, axis=1)

        matches = jnp.transpose(lax.map(one_plane, shifts[view_idx]), (1, 0, 2, 3)).astype(jnp.bfloat16)
        first_out = convolve(matches, conv_one, bias_one).astype(jnp.bfloat16)
        second_out = convolve(first_out, conv_two, bias_two)
        scores = jnp.einsum("c,cdhw->dhw", view_head, second_out)
        weight = jax.nn.sigmoid(scores)
        weighted = weighted + weight[None] * matches.astype(jnp.float32)
        total_weight = total_weight + weight
    return (weighted / total_weight[None]).astype(jnp.bfloat16)
```

```python
import functools
import numpy as np
import jax
import jax.numpy as jnp
from jax import lax
from jax.experimental import pallas as pl
from jax.experimental.pallas import tpu as pltpu

VIEWS = 4
F32 = jnp.float32
BF16 = jnp.bfloat16


def placing():
    table = np.zeros((4, 256, 384), np.float32)
    for ho in range(4):
        for a in range(3):
            for b in range(3):
                hi = ho + b - 1
                if not 0 <= hi < 4:
                    continue
                for e in range(3):
                    for i in range(8):
                        table[ho, (a * 9 + b * 3 + e) * 8 + i, a * 96 + e * 32 + i * 4 + hi] = 1
    return table.reshape(1024, 384)


def banded(w_ref, place_ref, out_ref, steps):
    flat = jnp.concatenate([w_ref[tap].astype(F32) for tap in range(27)], axis=1)
    flat = jnp.concatenate([flat, jnp.zeros((8, 40), F32)], axis=1).astype(BF16)
    row = lax.broadcasted_iota(jnp.int32, (32, 8), 0)
    col = lax.broadcasted_iota(jnp.int32, (32, 8), 1)
    spread = (row // 4 == col).astype(F32).astype(BF16)
    wide = jnp.dot(spread, flat, preferred_element_type=F32)
    which = lax.broadcasted_iota(jnp.int32, (32, 256), 0) % 4
    wide = jnp.concatenate(
        [jnp.where(which == ho, wide, 0.0) for ho in range(4)], axis=1
    ).astype(BF16)
    base = jnp.dot(wide, place_ref[...], preferred_element_type=F32)
    base = jnp.concatenate([base, jnp.zeros((32, 384), F32)], axis=1)
    for do in range(steps):
        out_ref[do * 32 : do * 32 + 32, :] = pltpu.roll(base, 96 * do, 1).astype(BF16) if do else base.astype(BF16)


def per_row(ref):
    low = lax.broadcasted_iota(jnp.int32, (8, 128), 0) < 4
    return [jnp.where(low, ref[2 * q], ref[2 * q + 1]) for q in range(4)]


def compute(
    plane_axis, tile_axis, sh, g_ref, l_ref, e_ref, r_ref, w1_ref, w2_ref, place_ref, b1_ref, b2_ref,
    head_ref, o_ref, src, rf, w1, w2, x, f, acc, tot,
):
    p = lax.axis_index(plane_axis)
    t = lax.axis_index(tile_axis)
    last_p = lax.axis_size(plane_axis) - 1
    last_t = lax.axis_size(tile_axis) - 1
    lane = lax.broadcasted_iota(jnp.int32, (8, 128), 1)
    lane32 = lax.broadcasted_iota(jnp.int32, (32, 128), 1)
    sub = lax.broadcasted_iota(jnp.int32, (8, 128), 0)
    low = sub < 4
    banded(w1_ref, place_ref, w1, 5)
    banded(w2_ref, place_ref, w2, 4)
    for k in range(3):
        rf[k] = r_ref[:, k * 128 : k * 128 + 128].astype(F32) * 0.25
    bias_one, bias_two, head = per_row(b1_ref), per_row(b2_ref), per_row(head_ref)
    edge_keep = jnp.where(
        jnp.logical_or(jnp.logical_and(lane == 0, t < last_t), jnp.logical_and(lane == 127, t > 0)), 1.0, 0.0
    )

    def neighbours(tiles, lanes):
        n = len(tiles)
        right = [pltpu.roll(a, 1, 1) for a in tiles]
        left = [pltpu.roll(a, 127, 1) for a in tiles]
        return (
            [jnp.where(lanes == 0, right[(k - 1) % n], right[k]) for k in range(n)],
            tiles,
            [jnp.where(lanes == 127, left[(k + 1) % n], left[k]) for k in range(n)],
        )

    def one_view(v, carry):
        own = pl.ds(pl.multiple_of(v * 16, 16), 16)
        src[0] = jnp.where(t > 0, l_ref[:, own, :].reshape(128, 128).astype(F32), 0.0)
        both = g_ref[:, own, :].reshape(128, 256).astype(F32)
        src[1] = both[:, :128]
        src[2] = both[:, 128:]
        src[3] = e_ref[:, v].reshape(128, 128).astype(F32)

        def one_plane(d, carry):
            s = sh[v, d]
            inside = jnp.logical_and(
                jnp.logical_or(d >= 2, p > 0), jnp.logical_or(d < 10, p < last_p)
            )
            scale = jnp.where(inside, 1.0, 0.0)
            before = lane32 < s
            parts = [[], [], []]
            for q in range(4):
                rows = slice(32 * q, 32 * q + 32)
                r = [pltpu.roll(src[k, rows, :], s, 1) for k in range(4)]
                tiles = (
                    jnp.where(before, r[0], r[1]),
                    jnp.where(before, r[1], r[2]),
                    jnp.where(
                        lane32 < 64, jnp.where(before, r[2], r[3]), jnp.where(before, r[3], r[0])
                    ),
                )
                for k in range(3):
                    prod = tiles[k] * rf[k, rows, :]
                    v0 = prod[0:8] + prod[8:16]
                    v1 = prod[16:24] + prod[24:32]
                    both = jnp.where(low, v0, v1) + pltpu.roll(jnp.where(low, v1, v0), 4, 0)
                    parts[k].append(both * scale)
            tiles = [jnp.concatenate(parts[k], axis=0) for k in range(3)]
            base = pl.multiple_of(d * 96, 32)
            for e, moved in enumerate(neighbours(tiles, lane32)):
                for k in range(3):
                    x[pl.ds(base + e * 32, 32), k * 128 : k * 128 + 128] = moved[k].astype(BF16)
            return carry

        lax.fori_loop(0, 12, one_plane, 0, unroll=2)

        for j in range(2):
            raw = jnp.dot(
                w1[:, :672], x[j * 480 : j * 480 + 672, :], preferred_element_type=F32
            )
            for i in range(5):
                d = j * 5 + i
                tiles = []
                for k in range(3):
                    cols = slice(k * 128, k * 128 + 128)
                    rows = []
                    for q in range(4):
                        at = i * 32 + q * 8
                        val = jnp.maximum(raw[at : at + 8, cols] + bias_one[q], 0.0)
                        if k == 2:
                            val = val * edge_keep
                        if d == 0:
                            val = jnp.where(p > 0, val, 0.0)
                        if d == 9:
                            val = jnp.where(p < last_p, val, 0.0)
                        rows.append(val)
                    tiles.append(jnp.concatenate(rows, axis=0))
                for e, moved in enumerate(neighbours(tiles, lane32)):
                    for k in range(2):
                        f[d * 96 + e * 32 : d * 96 + e * 32 + 32, k * 128 : k * 128 + 128] = moved[k].astype(BF16)

        for j in range(2):
            raw = jnp.dot(w2[:, :576], f[j * 384 : j * 384 + 576, :], preferred_element_type=F32)
            for i in range(4):
                d = j * 4 + i
                for k in range(2):
                    cols = slice(k * 128, k * 128 + 128)
                    score = None
                    for q in range(4):
                        at = i * 32 + q * 8
                        term = jnp.maximum(raw[at : at + 8, cols] + bias_two[q], 0.0) * head[q]
                        score = term if score is None else score + term
                    score = score + pltpu.roll(score, 4, 0)
                    weight = 1.0 / (1.0 + jnp.exp(-score))
                    at = (d + 2) * 96 + 32
                    match = x[at : at + 32, cols].astype(F32)
                    tot[d, :, cols] = tot[d, :, cols] + weight
                    for q in range(4):
                        rows = slice(q * 8, q * 8 + 8)
                        acc[d, rows, cols] = acc[d, rows, cols] + weight * match[rows]
        return carry

    acc[...] = jnp.zeros_like(acc)
    tot[...] = jnp.zeros_like(tot)
    lax.fori_loop(0, VIEWS, one_view, 0)
    for d in range(8):
        for q in range(4):
            val = (acc[d, q * 8 : q * 8 + 8, :] / tot[d]).astype(BF16)
            o_ref[2 * q, d] = val[0:4]
            o_ref[2 * q + 1, d] = val[4:8]


def call_compute(plane_axis, tile_axis, sh, g, l, e, r, w1, w2, b1, b2, head):
    smem = pl.BlockSpec(memory_space=pltpu.SMEM)
    vmem = pl.BlockSpec(memory_space=pltpu.VMEM)
    place = jnp.asarray(placing(), BF16)
    return pl.pallas_call(
        functools.partial(compute, plane_axis, tile_axis),
        out_shape=jax.ShapeDtypeStruct((8, 8, 4, 256), BF16),
        in_specs=[smem, vmem, vmem, vmem, vmem, vmem, vmem, vmem, smem, smem, smem],
        out_specs=vmem,
        scratch_shapes=[
            pltpu.VMEM((4, 128, 128), F32),
            pltpu.VMEM((3, 128, 128), F32),
            pltpu.VMEM((160, 768), BF16),
            pltpu.VMEM((128, 768), BF16),
            pltpu.VMEM((1152, 384), BF16),
            pltpu.VMEM((960, 256), BF16),
            pltpu.VMEM((8, 32, 256), F32),
            pltpu.VMEM((8, 8, 256), F32),
        ],
        compiler_params=pltpu.CompilerParams(vmem_limit_bytes=40 << 20),
        name="cost_volume",
    )(sh, g, l, e, r, w1, w2, place, b1, b2, head)


MESH = pl.DeviceIdType.MESH


def exchange(pack_ref, g_ref, l_ref, r_ref, send, recv, pass_send, pass_recv, own_sem):
    t, p = lax.axis_index("tile"), lax.axis_index("plane")
    last = lax.axis_size("tile") - 1
    chip, core = p // 2, p % 2
    other = chip * 2 + 1 - core
    peers = [other] + [(chip + dz) % 4 * 2 + core for dz in range(1, 4)]
    sources = [other] + [(chip + 4 - dz) % 4 * 2 + core for dz in range(1, 4)]

    barrier = pltpu.get_barrier_semaphore()

    def greet(tile, plane):
        pl.semaphore_signal(barrier, inc=1, device_id=(tile, plane), device_id_type=MESH)

    @pl.when(t < last)
    def _():
        greet(t + 1, p)

    @pl.when(t > 0)
    def _():
        greet(t - 1, p)

    for dz in range(4):
        greet(t, peers[dz])

    sides = jnp.where(t < last, 1, 0) + jnp.where(t > 0, 1, 0)
    pl.semaphore_wait(barrier, 4 + sides)

    def copy(src, dst, from_sem, to_sem, tile, plane):
        return pltpu.make_async_remote_copy(
            src_ref=src, dst_ref=dst, send_sem=from_sem, recv_sem=to_sem,
            device_id=(tile, plane), device_id_type=MESH,
        )

    right = copy(pack_ref.at[:, 128:256], l_ref.at[p], send.at[0, 4], recv.at[0, 4], t + 1, p)
    left = copy(pack_ref.at[64:72, 0:128], r_ref.at[p], send.at[1, 4], recv.at[1, 4], t - 1, p)
    bufs = (g_ref, l_ref, r_ref)

    def spread(kind, dz):
        src = pack_ref if kind == 0 else bufs[kind].at[p]
        return copy(src, bufs[kind].at[p], send.at[kind, dz], recv.at[kind, dz], t, peers[dz])

    def passing(kind, dz):
        slot = bufs[kind].at[sources[dz]]
        return copy(slot, slot, pass_send.at[kind, dz], pass_recv.at[kind, dz], t, other)

    mine = pltpu.make_async_copy(pack_ref, g_ref.at[p], own_sem)

    @pl.when(t < last)
    def _():
        right.start()

    @pl.when(t > 0)
    def _():
        left.start()

    for dz in (2, 1, 3, 0):
        spread(0, dz).start()
    mine.start()

    @pl.when(t > 0)
    def _():
        right.wait_recv()
        for dz in (2, 1, 3, 0):
            spread(1, dz).start()

    @pl.when(t < last)
    def _():
        left.wait_recv()
        for dz in (2, 1, 3, 0):
            spread(2, dz).start()

    def relay(kind):
        for dz in (1, 3, 2):
            spread(kind, dz).wait_recv()
            passing(kind, dz).start()

    def finish(kind):
        spread(kind, 0).wait_recv()
        for dz in range(4):
            spread(kind, dz).wait_send()
        for dz in (1, 3, 2):
            passing(kind, dz).wait()

    relay(0)

    @pl.when(t > 0)
    def _():
        relay(1)

    @pl.when(t < last)
    def _():
        relay(2)

    mine.wait()
    finish(0)

    @pl.when(t > 0)
    def _():
        finish(1)
        left.wait_send()

    @pl.when(t < last)
    def _():
        finish(2)
        right.wait_send()


def call_exchange(pack):
    vmem = pl.BlockSpec(memory_space=pltpu.VMEM)
    return pl.pallas_call(
        exchange,
        out_shape=[
            jax.ShapeDtypeStruct((8, 72, 256), BF16),
            jax.ShapeDtypeStruct((8, 72, 128), BF16),
            jax.ShapeDtypeStruct((8, 8, 128), BF16),
        ],
        in_specs=[vmem],
        out_specs=[vmem, vmem, vmem],
        scratch_shapes=[
            pltpu.SemaphoreType.DMA((3, 5)),
            pltpu.SemaphoreType.DMA((3, 5)),
            pltpu.SemaphoreType.DMA((3, 4)),
            pltpu.SemaphoreType.DMA((3, 4)),
            pltpu.SemaphoreType.DMA,
        ],
        compiler_params=pltpu.CompilerParams(
            collective_id=0, has_side_effects=True, vmem_limit_bytes=8 << 20
        ),
        name="exchange",
    )(pack)


def per_device(ref_feat, src_feat, shifts, conv_one, bias_one, conv_two, bias_two, view_head):
    t, p = lax.axis_index("tile"), lax.axis_index("plane")
    last_t = lax.axis_size("tile") - 1
    ref_rows = ref_feat.reshape(128, 256)
    src_rows = src_feat.reshape(64, 256)

    def side(at, more):
        lo = jnp.pad(src_rows[:, at : at + 2].T, ((0, 0), (0, 64)))
        at = at if at == 0 else 254
        hi = ref_rows[:, at : at + 2].T
        return jnp.concatenate([lo, hi, more], axis=0)

    whole = jnp.pad(shifts.reshape(1, 32).astype(BF16), ((0, 3), (0, 96)))
    extra = jnp.concatenate([side(0, whole), side(126, jnp.zeros((4, 128), BF16))], axis=1)
    pack = jnp.concatenate([src_rows, extra], axis=0)
    g, l, r = call_exchange(pack)

    def columns(rows):
        return jnp.transpose(rows.reshape(8, 2, 4, 16), (0, 2, 3, 1))

    el = columns(jnp.where(t > 0, l[:, 64:66, :64], 0))
    er = columns(jnp.where(t < last_t, r[:, 0:2, :64], 0))
    e = jnp.concatenate([er, jnp.zeros((8, 4, 16, 124), BF16), el], axis=-1)
    rl = jnp.where(t > 0, l[0, 66:68, :], 0).T
    rr = jnp.where(t < last_t, r[0, 2:4, :], 0).T
    ref_wide = jnp.concatenate([ref_rows, rr, jnp.zeros((128, 124), BF16), rl], axis=1)
    every = g[:, 68, :32].astype(jnp.int32).reshape(8, 4, 8)
    every = jnp.pad(jnp.transpose(every, (1, 0, 2)).reshape(4, 64), ((0, 0), (2, 2)))
    sh = lax.dynamic_slice_in_dim(every, p * 8, 12, 1)
    kernel_of = lambda w: jnp.transpose(w, (2, 3, 4, 0, 1)).reshape(27, 8, 8)
    return call_compute(
        "plane", "tile", sh, g, l, e, ref_wide,
        kernel_of(conv_one), kernel_of(conv_two), bias_one, bias_two, view_head,
    )


def solution(mesh):
    from jax.sharding import PartitionSpec as P
    placed = (
        P(None, None, "tile"), P(None, "plane", None, "tile"), P(None, "plane"),
        P(), P(), P(), P(), P(),
    )
    return jax.shard_map(
        per_device, mesh=mesh, in_specs=placed, out_specs=P(None, "plane", None, "tile"), check_vma=False,
    )
```

```python
import functools
import numpy as np
import jax
import jax.numpy as jnp
from jax import lax
from jax.experimental import pallas as pl
from jax.experimental.pallas import tpu as pltpu

VIEWS = 4
F32 = jnp.float32
BF16 = jnp.bfloat16


def placing():
    table = np.zeros((4, 256, 384), np.float32)
    for ho in range(4):
        for a in range(3):
            for b in range(3):
                hi = ho + b - 1
                if not 0 <= hi < 4:
                    continue
                for e in range(3):
                    for i in range(8):
                        table[ho, (a * 9 + b * 3 + e) * 8 + i, a * 96 + e * 32 + i * 4 + hi] = 1
    return table.reshape(1024, 384)


def banded(w_ref, place_ref, out_ref, steps):
    flat = jnp.concatenate([w_ref[tap].astype(F32) for tap in range(27)], axis=1)
    flat = jnp.concatenate([flat, jnp.zeros((8, 40), F32)], axis=1).astype(BF16)
    row = lax.broadcasted_iota(jnp.int32, (32, 8), 0)
    col = lax.broadcasted_iota(jnp.int32, (32, 8), 1)
    spread = (row // 4 == col).astype(F32).astype(BF16)
    wide = jnp.dot(spread, flat, preferred_element_type=F32)
    which = lax.broadcasted_iota(jnp.int32, (32, 256), 0) % 4
    wide = jnp.concatenate(
        [jnp.where(which == ho, wide, 0.0) for ho in range(4)], axis=1
    ).astype(BF16)
    base = jnp.dot(wide, place_ref[...], preferred_element_type=F32)
    base = jnp.concatenate([base, jnp.zeros((32, 384), F32)], axis=1)
    for do in range(steps):
        out_ref[do * 32 : do * 32 + 32, :] = pltpu.roll(base, 96 * do, 1).astype(BF16) if do else base.astype(BF16)


def per_row(ref):
    low = lax.broadcasted_iota(jnp.int32, (8, 128), 0) < 4
    return [jnp.where(low, ref[2 * q], ref[2 * q + 1]) for q in range(4)]


def compute(
    plane_axis, tile_axis, sh, g_ref, l_ref, e_ref, r_ref, w1_ref, w2_ref, place_ref, b1_ref, b2_ref,
    head_ref, o_ref, src2, rf, w1, w2, x2, f2, acc, tot,
):
    p = lax.axis_index(plane_axis)
    t = lax.axis_index(tile_axis)
    last_p = lax.axis_size(plane_axis) - 1
    last_t = lax.axis_size(tile_axis) - 1
    lane = lax.broadcasted_iota(jnp.int32, (8, 128), 1)
    lane32 = lax.broadcasted_iota(jnp.int32, (32, 128), 1)
    sub = lax.broadcasted_iota(jnp.int32, (8, 128), 0)
    low = sub < 4
    banded(w1_ref, place_ref, w1, 5)
    banded(w2_ref, place_ref, w2, 4)
    for k in range(3):
        rf[k] = r_ref[:, k * 128 : k * 128 + 128].astype(F32) * 0.25
    bias_one, bias_two, head = per_row(b1_ref), per_row(b2_ref), per_row(head_ref)
    edge_keep = jnp.where(
        jnp.logical_or(jnp.logical_and(lane == 0, t < last_t), jnp.logical_and(lane == 127, t > 0)), 1.0, 0.0
    )

    def neighbours(tiles, lanes):
        n = len(tiles)
        tiles = [a.astype(BF16) for a in tiles]
        right = [pltpu.roll(a, 1, 1) for a in tiles]
        left = [pltpu.roll(a, 127, 1) for a in tiles]
        return (
            [jnp.where(lanes == 0, right[(k - 1) % n], right[k]) for k in range(n)],
            tiles,
            [jnp.where(lanes == 127, left[(k + 1) % n], left[k]) for k in range(n)],
        )

    def one_view(v, xs, f):
        x, src = xs, src2
        own = pl.ds(pl.multiple_of(v * 16, 16), 16)
        src[0] = jnp.where(t > 0, l_ref[:, own, :].reshape(128, 128), jnp.zeros((128, 128), BF16))
        both = g_ref[:, own, :].reshape(128, 256)
        src[1] = both[:, :128]
        src[2] = both[:, 128:]
        src[3] = e_ref[:, v].reshape(128, 128)

        def one_plane(d):
            s = sh[v, d]
            before = lane32 < s
            outer = jnp.logical_xor(before, lane32 < 64)
            parts = [[], [], []]
            for q in range(4):
                rows = slice(32 * q, 32 * q + 32)
                r = [pltpu.roll(src[k, rows, :], s, 1) for k in range(4)]
                tiles = (
                    jnp.where(before, r[0], r[1]),
                    jnp.where(before, r[1], r[2]),
                    jnp.where(outer, r[3], jnp.where(lane32 < 64, r[2], r[0])),
                )
                for k in range(3):
                    prod = tiles[k].astype(F32) * rf[k, rows, :]
                    v0 = prod[0:8] + prod[8:16]
                    v1 = prod[16:24] + prod[24:32]
                    both = jnp.where(low, v0, v1) + pltpu.roll(jnp.where(low, v1, v0), 4, 0)
                    parts[k].append(both)
            tiles = [jnp.concatenate(parts[k], axis=0) for k in range(3)]
            if d < 2:
                tiles = [jnp.where(p > 0, a, 0.0) for a in tiles]
            if d > 9:
                tiles = [jnp.where(p < last_p, a, 0.0) for a in tiles]
            base = d * 96
            for e, moved in enumerate(neighbours(tiles, lane32)):
                for k in range(3):
                    x[base + e * 32 : base + e * 32 + 32, k * 128 : k * 128 + 128] = moved[k]

        for d in range(12):
            one_plane(d)

        for j in range(2):
            raw = jnp.dot(
                w1[:, :672], x[j * 480 : j * 480 + 672, :], preferred_element_type=F32
            )
            for i in range(5):
                d = j * 5 + i
                tiles = []
                for k in range(3):
                    cols = slice(k * 128, k * 128 + 128)
                    rows = []
                    for q in range(4):
                        at = i * 32 + q * 8
                        val = jnp.maximum(raw[at : at + 8, cols] + bias_one[q], 0.0)
                        if k == 2:
                            val = val * edge_keep
                        if d == 0:
                            val = jnp.where(p > 0, val, 0.0)
                        if d == 9:
                            val = jnp.where(p < last_p, val, 0.0)
                        rows.append(val)
                    tiles.append(jnp.concatenate(rows, axis=0))
                for e, moved in enumerate(neighbours(tiles, lane32)):
                    for k in range(2):
                        f[d * 96 + e * 32 : d * 96 + e * 32 + 32, k * 128 : k * 128 + 128] = moved[k]

        for j in range(2):
            raw = jnp.dot(w2[:, :576], f[j * 384 : j * 384 + 576, :], preferred_element_type=F32)
            for i in range(4):
                d = j * 4 + i
                for k in range(2):
                    cols = slice(k * 128, k * 128 + 128)
                    score = None
                    for q in range(4):
                        at = i * 32 + q * 8
                        term = jnp.maximum(raw[at : at + 8, cols] + bias_two[q], 0.0) * head[q]
                        score = term if score is None else score + term
                    score = score + pltpu.roll(score, 4, 0)
                    weight = 1.0 / (1.0 + jnp.exp(-score))
                    at = (d + 2) * 96 + 32
                    match = x[at : at + 32, cols].astype(F32)
                    tot[d, :, cols] = tot[d, :, cols] + weight
                    for q in range(4):
                        rows = slice(q * 8, q * 8 + 8)
                        acc[d, rows, cols] = acc[d, rows, cols] + weight * match[rows]

    def two_views(i, carry):
        for k in range(2):
            one_view(i * 2 + k, x2.at[k], f2.at[k])
        return carry

    acc[...] = jnp.zeros_like(acc)
    tot[...] = jnp.zeros_like(tot)
    two_views(0, 0)
    two_views(1, 0)
    for d in range(8):
        for q in range(4):
            val = (acc[d, q * 8 : q * 8 + 8, :] / tot[d]).astype(BF16)
            o_ref[2 * q, d] = val[0:4]
            o_ref[2 * q + 1, d] = val[4:8]


def call_compute(plane_axis, tile_axis, sh, g, l, e, r, w1, w2, b1, b2, head):
    smem = pl.BlockSpec(memory_space=pltpu.SMEM)
    vmem = pl.BlockSpec(memory_space=pltpu.VMEM)
    place = jnp.asarray(placing(), BF16)
    return pl.pallas_call(
        functools.partial(compute, plane_axis, tile_axis),
        out_shape=jax.ShapeDtypeStruct((8, 8, 4, 256), BF16),
        in_specs=[smem, vmem, vmem, vmem, vmem, vmem, vmem, vmem, smem, smem, smem],
        out_specs=vmem,
        scratch_shapes=[
            pltpu.VMEM((4, 128, 128), BF16),
            pltpu.VMEM((3, 128, 128), F32),
            pltpu.VMEM((160, 768), BF16),
            pltpu.VMEM((128, 768), BF16),
            pltpu.VMEM((2, 1152, 384), BF16),
            pltpu.VMEM((2, 960, 256), BF16),
            pltpu.VMEM((8, 32, 256), F32),
            pltpu.VMEM((8, 8, 256), F32),
        ],
        compiler_params=pltpu.CompilerParams(vmem_limit_bytes=40 << 20),
        name="cost_volume",
    )(sh, g, l, e, r, w1, w2, place, b1, b2, head)


MESH = pl.DeviceIdType.MESH


def exchange(pack_ref, g_ref, l_ref, r_ref, send, recv, pass_send, pass_recv, own_sem):
    t, p = lax.axis_index("tile"), lax.axis_index("plane")
    last = lax.axis_size("tile") - 1
    chip, core = p // 2, p % 2
    other = chip * 2 + 1 - core
    peers = [other] + [(chip + dz) % 4 * 2 + core for dz in range(1, 4)]
    sources = [other] + [(chip + 4 - dz) % 4 * 2 + core for dz in range(1, 4)]

    barrier = pltpu.get_barrier_semaphore()

    def greet(tile, plane):
        pl.semaphore_signal(barrier, inc=1, device_id=(tile, plane), device_id_type=MESH)

    @pl.when(t < last)
    def _():
        greet(t + 1, p)

    @pl.when(t > 0)
    def _():
        greet(t - 1, p)

    for dz in range(4):
        greet(t, peers[dz])

    sides = jnp.where(t < last, 1, 0) + jnp.where(t > 0, 1, 0)
    pl.semaphore_wait(barrier, 4 + sides)

    def copy(src, dst, from_sem, to_sem, tile, plane):
        return pltpu.make_async_remote_copy(
            src_ref=src, dst_ref=dst, send_sem=from_sem, recv_sem=to_sem,
            device_id=(tile, plane), device_id_type=MESH,
        )

    right = copy(pack_ref.at[:, 128:256], l_ref.at[p], send.at[0, 4], recv.at[0, 4], t + 1, p)
    left = copy(pack_ref.at[64:72, 0:128], r_ref.at[p], send.at[1, 4], recv.at[1, 4], t - 1, p)
    bufs = (g_ref, l_ref, r_ref)

    def spread(kind, dz):
        src = pack_ref if kind == 0 else bufs[kind].at[p]
        return copy(src, bufs[kind].at[p], send.at[kind, dz], recv.at[kind, dz], t, peers[dz])

    def passing(kind, dz):
        slot = bufs[kind].at[sources[dz]]
        return copy(slot, slot, pass_send.at[kind, dz], pass_recv.at[kind, dz], t, other)

    mine = pltpu.make_async_copy(pack_ref, g_ref.at[p], own_sem)

    @pl.when(t < last)
    def _():
        right.start()

    @pl.when(t > 0)
    def _():
        left.start()

    for dz in (2, 1, 3, 0):
        spread(0, dz).start()
    mine.start()

    @pl.when(t > 0)
    def _():
        right.wait_recv()
        for dz in (2, 1, 3, 0):
            spread(1, dz).start()

    @pl.when(t < last)
    def _():
        left.wait_recv()
        for dz in (2, 1, 3, 0):
            spread(2, dz).start()

    def relay(kind):
        for dz in (1, 3, 2):
            spread(kind, dz).wait_recv()
            passing(kind, dz).start()

    def finish(kind):
        spread(kind, 0).wait_recv()
        for dz in range(4):
            spread(kind, dz).wait_send()
        for dz in (1, 3, 2):
            passing(kind, dz).wait()

    relay(0)

    @pl.when(t > 0)
    def _():
        relay(1)

    @pl.when(t < last)
    def _():
        relay(2)

    mine.wait()
    finish(0)

    @pl.when(t > 0)
    def _():
        finish(1)
        left.wait_send()

    @pl.when(t < last)
    def _():
        finish(2)
        right.wait_send()


def call_exchange(pack):
    vmem = pl.BlockSpec(memory_space=pltpu.VMEM)
    return pl.pallas_call(
        exchange,
        out_shape=[
            jax.ShapeDtypeStruct((8, 72, 256), BF16),
            jax.ShapeDtypeStruct((8, 72, 128), BF16),
            jax.ShapeDtypeStruct((8, 8, 128), BF16),
        ],
        in_specs=[vmem],
        out_specs=[vmem, vmem, vmem],
        scratch_shapes=[
            pltpu.SemaphoreType.DMA((3, 5)),
            pltpu.SemaphoreType.DMA((3, 5)),
            pltpu.SemaphoreType.DMA((3, 4)),
            pltpu.SemaphoreType.DMA((3, 4)),
            pltpu.SemaphoreType.DMA,
        ],
        compiler_params=pltpu.CompilerParams(
            collective_id=0, has_side_effects=True, vmem_limit_bytes=8 << 20
        ),
        name="exchange",
    )(pack)


def per_device(ref_feat, src_feat, shifts, conv_one, bias_one, conv_two, bias_two, view_head):
    t, p = lax.axis_index("tile"), lax.axis_index("plane")
    last_t = lax.axis_size("tile") - 1
    ref_rows = ref_feat.reshape(128, 256)
    src_rows = src_feat.reshape(64, 256)

    def side(at, more):
        lo = jnp.pad(src_rows[:, at : at + 2].T, ((0, 0), (0, 64)))
        at = at if at == 0 else 254
        hi = ref_rows[:, at : at + 2].T
        return jnp.concatenate([lo, hi, more], axis=0)

    whole = jnp.pad(shifts.reshape(1, 32).astype(BF16), ((0, 3), (0, 96)))
    extra = jnp.concatenate([side(0, whole), side(126, jnp.zeros((4, 128), BF16))], axis=1)
    pack = jnp.concatenate([src_rows, extra], axis=0)
    g, l, r = call_exchange(pack)

    def columns(rows):
        return jnp.transpose(rows.reshape(8, 2, 4, 16), (0, 2, 3, 1))

    el = columns(jnp.where(t > 0, l[:, 64:66, :64], 0))
    er = columns(jnp.where(t < last_t, r[:, 0:2, :64], 0))
    e = jnp.concatenate([er, jnp.zeros((8, 4, 16, 124), BF16), el], axis=-1)
    rl = jnp.where(t > 0, l[0, 66:68, :], 0).T
    rr = jnp.where(t < last_t, r[0, 2:4, :], 0).T
    ref_wide = jnp.concatenate([ref_rows, rr, jnp.zeros((128, 124), BF16), rl], axis=1)
    every = g[:, 68, :32].astype(jnp.int32).reshape(8, 4, 8)
    every = jnp.pad(jnp.transpose(every, (1, 0, 2)).reshape(4, 64), ((0, 0), (2, 2)))
    sh = lax.dynamic_slice_in_dim(every, p * 8, 12, 1)
    kernel_of = lambda w: jnp.transpose(w, (2, 3, 4, 0, 1)).reshape(27, 8, 8)
    return call_compute(
        "plane", "tile", sh, g, l, e, ref_wide,
        kernel_of(conv_one), kernel_of(conv_two), bias_one, bias_two, view_head,
    )


def solution(mesh):
    from jax.sharding import PartitionSpec as P
    placed = (
        P(None, None, "tile"), P(None, "plane", None, "tile"), P(None, "plane"),
        P(), P(), P(), P(), P(),
    )
    return jax.shard_map(
        per_device, mesh=mesh, in_specs=placed, out_specs=P(None, "plane", None, "tile"), check_vma=False,
    )
```

```python
import functools
import numpy as np
import jax
import jax.numpy as jnp
from jax import lax
from jax.experimental import pallas as pl
from jax.experimental.pallas import tpu as pltpu

VIEWS = 4
F32 = jnp.float32
BF16 = jnp.bfloat16


def placing():
    table = np.zeros((4, 256, 384), np.float32)
    for ho in range(4):
        for a in range(3):
            for b in range(3):
                hi = ho + b - 1
                if not 0 <= hi < 4:
                    continue
                for e in range(3):
                    for i in range(8):
                        table[ho, (a * 9 + b * 3 + e) * 8 + i, a * 96 + e * 32 + i * 4 + hi] = 1
    return table.reshape(1024, 384)


def banded(w_ref, place_ref, out_ref, steps):
    flat = jnp.concatenate([w_ref[tap].astype(F32) for tap in range(27)], axis=1)
    flat = jnp.concatenate([flat, jnp.zeros((8, 40), F32)], axis=1).astype(BF16)
    row = lax.broadcasted_iota(jnp.int32, (32, 8), 0)
    col = lax.broadcasted_iota(jnp.int32, (32, 8), 1)
    spread = (row // 4 == col).astype(F32).astype(BF16)
    wide = jnp.dot(spread, flat, preferred_element_type=F32)
    which = lax.broadcasted_iota(jnp.int32, (32, 256), 0) % 4
    wide = jnp.concatenate(
        [jnp.where(which == ho, wide, 0.0) for ho in range(4)], axis=1
    ).astype(BF16)
    base = jnp.dot(wide, place_ref[...], preferred_element_type=F32)
    base = jnp.concatenate([base, jnp.zeros((32, 384), F32)], axis=1)
    for do in range(steps):
        out_ref[do * 32 : do * 32 + 32, :] = pltpu.roll(base, 96 * do, 1).astype(BF16) if do else base.astype(BF16)


def per_row(ref, k):
    low = lax.broadcasted_iota(jnp.int32, (8, 128), 0) < 4
    return [jnp.where(low, ref[k, 0, 2 * q], ref[k, 0, 2 * q + 1]) for q in range(4)]


def compute(
    plane_axis, tile_axis, small, sh, g_ref, l_ref, e_ref, r_ref, w1, w2, o_ref,
    src2, rf, x2, f2, acc, tot,
):
    p = lax.axis_index(plane_axis)
    t = lax.axis_index(tile_axis)
    last_p = lax.axis_size(plane_axis) - 1
    last_t = lax.axis_size(tile_axis) - 1
    lane = lax.broadcasted_iota(jnp.int32, (8, 128), 1)
    lane32 = lax.broadcasted_iota(jnp.int32, (32, 128), 1)
    sub = lax.broadcasted_iota(jnp.int32, (8, 128), 0)
    low = sub < 4
    for k in range(3):
        rf[k] = r_ref[:, k * 128 : k * 128 + 128].astype(F32) * 0.25
    bias_one, bias_two, head = per_row(small, 0), per_row(small, 1), per_row(small, 2)
    edge_keep = jnp.where(
        jnp.logical_or(jnp.logical_and(lane == 0, t < last_t), jnp.logical_and(lane == 127, t > 0)), 1.0, 0.0
    )

    def neighbours(tiles, lanes):
        n = len(tiles)
        tiles = [a.astype(BF16) for a in tiles]
        right = [pltpu.roll(a, 1, 1) for a in tiles]
        left = [pltpu.roll(a, 127, 1) for a in tiles]
        return (
            [jnp.where(lanes == 0, right[(k - 1) % n], right[k]) for k in range(n)],
            tiles,
            [jnp.where(lanes == 127, left[(k + 1) % n], left[k]) for k in range(n)],
        )

    def one_view(v, xs, f):
        x, src = xs, src2
        own = pl.ds(pl.multiple_of(v * 16, 16), 16)
        src[0] = jnp.where(t > 0, l_ref[:, own, :].reshape(128, 128), jnp.zeros((128, 128), BF16))
        both = g_ref[:, own, :].reshape(128, 256)
        src[1] = both[:, :128]
        src[2] = both[:, 128:]
        src[3] = e_ref[:, own, :].reshape(128, 128)

        def one_plane(d):
            if d < 2:
                s = sh[jnp.maximum(p - 1, 0) * 8 + 4 + v, 6 + d]
            elif d > 9:
                s = sh[jnp.minimum(p + 1, last_p) * 8 + 4 + v, d - 10]
            else:
                s = sh[p * 8 + 4 + v, d - 2]
            before = lane32 < s
            outer = jnp.logical_xor(before, lane32 < 64)
            parts = [[], [], []]
            for q in range(4):
                rows = slice(32 * q, 32 * q + 32)
                r = [pltpu.roll(src[k, rows, :], s, 1) for k in range(4)]
                tiles = (
                    jnp.where(before, r[0], r[1]),
                    jnp.where(before, r[1], r[2]),
                    jnp.where(outer, r[3], jnp.where(lane32 < 64, r[2], r[0])),
                )
                for k in range(3):
                    prod = tiles[k].astype(F32) * rf[k, rows, :]
                    v0 = prod[0:8] + prod[8:16]
                    v1 = prod[16:24] + prod[24:32]
                    both = jnp.where(low, v0, v1) + pltpu.roll(jnp.where(low, v1, v0), 4, 0)
                    parts[k].append(both)
            tiles = [jnp.concatenate(parts[k], axis=0) for k in range(3)]
            if d < 2:
                tiles = [jnp.where(p > 0, a, 0.0) for a in tiles]
            if d > 9:
                tiles = [jnp.where(p < last_p, a, 0.0) for a in tiles]
            base = d * 96
            for e, moved in enumerate(neighbours(tiles, lane32)):
                for k in range(3):
                    x[base + e * 32 : base + e * 32 + 32, k * 128 : k * 128 + 128] = moved[k]

        for d in range(12):
            one_plane(d)

        for j in range(2):
            raw = jnp.dot(
                w1[:, :672], x[j * 480 : j * 480 + 672, :], preferred_element_type=F32
            )
            for i in range(5):
                d = j * 5 + i
                tiles = []
                for k in range(3):
                    cols = slice(k * 128, k * 128 + 128)
                    rows = []
                    for q in range(4):
                        at = i * 32 + q * 8
                        val = jnp.maximum(raw[at : at + 8, cols] + bias_one[q], 0.0)
                        if k == 2:
                            val = val * edge_keep
                        if d == 0:
                            val = jnp.where(p > 0, val, 0.0)
                        if d == 9:
                            val = jnp.where(p < last_p, val, 0.0)
                        rows.append(val)
                    tiles.append(jnp.concatenate(rows, axis=0))
                for e, moved in enumerate(neighbours(tiles, lane32)):
                    for k in range(2):
                        f[d * 96 + e * 32 : d * 96 + e * 32 + 32, k * 128 : k * 128 + 128] = moved[k]

        for j in range(2):
            raw = jnp.dot(w2[:, :576], f[j * 384 : j * 384 + 576, :], preferred_element_type=F32)
            for i in range(4):
                d = j * 4 + i
                for k in range(2):
                    cols = slice(k * 128, k * 128 + 128)
                    score = None
                    for q in range(4):
                        at = i * 32 + q * 8
                        term = jnp.maximum(raw[at : at + 8, cols] + bias_two[q], 0.0) * head[q]
                        score = term if score is None else score + term
                    score = score + pltpu.roll(score, 4, 0)
                    weight = 1.0 / (1.0 + jnp.exp(-score))
                    at = (d + 2) * 96 + 32
                    match = x[at : at + 32, cols].astype(F32)
                    tot[d, :, cols] = tot[d, :, cols] + weight
                    for q in range(4):
                        rows = slice(q * 8, q * 8 + 8)
                        acc[d, rows, cols] = acc[d, rows, cols] + weight * match[rows]

    def two_views(i, carry):
        for k in range(2):
            one_view(i * 2 + k, x2.at[k], f2.at[k])
        return carry

    acc[...] = jnp.zeros_like(acc)
    tot[...] = jnp.zeros_like(tot)
    two_views(0, 0)
    two_views(1, 0)
    for d in range(8):
        for q in range(4):
            val = (acc[d, q * 8 : q * 8 + 8, :] / tot[d]).astype(BF16)
            o_ref[2 * q, d] = val[0:4]
            o_ref[2 * q + 1, d] = val[4:8]


def call_compute(plane_axis, tile_axis, small, sh, g, l, e, r, w1, w2):
    smem = pl.BlockSpec(memory_space=pltpu.SMEM)
    vmem = pl.BlockSpec(memory_space=pltpu.VMEM)
    return pl.pallas_call(
        functools.partial(compute, plane_axis, tile_axis),
        out_shape=jax.ShapeDtypeStruct((8, 8, 4, 256), BF16),
        in_specs=[smem, smem] + [vmem] * 6,
        out_specs=vmem,
        scratch_shapes=[
            pltpu.VMEM((4, 128, 128), BF16),
            pltpu.VMEM((3, 128, 128), F32),
            pltpu.VMEM((2, 1152, 384), BF16),
            pltpu.VMEM((2, 960, 256), BF16),
            pltpu.VMEM((8, 32, 256), F32),
            pltpu.VMEM((8, 8, 256), F32),
        ],
        compiler_params=pltpu.CompilerParams(vmem_limit_bytes=60 * 1024 * 1024),
        name="cost_volume",
    )(small, sh, g, l, e, r, w1, w2)


MESH = pl.DeviceIdType.MESH


def marks(rows, pairs):
    row = lax.broadcasted_iota(jnp.int32, (rows, 128), 0)
    lane = lax.broadcasted_iota(jnp.int32, (rows, 128), 1)
    hit = None
    for r, l in pairs:
        here = jnp.logical_and(row == r, lane == l)
        hit = here if hit is None else jnp.logical_or(hit, here)
    return jnp.where(hit, 1.0, 0.0).astype(BF16)


def pick(mark, rows):
    return lax.dot_general(mark, rows, (((1,), (1,)), ((), ())), preferred_element_type=F32)


def unpick(rows, mark):
    return lax.dot_general(rows, mark, (((0,), (0,)), ((), ())), preferred_element_type=F32)


def exchange(
    src_hbm, ref_hbm, sh_hbm, w1_hbm, w2_hbm, b1_hbm, b2_hbm, head_hbm, place_hbm, small_out, sh_out, g_ref, l_ref, e_ref, wide_ref, w1_out, w2_out,
    src_raw, ref_raw, sh_ref, w_raw, place, pack_ref, r_ref, send, recv, pass_send, pass_recv, own_sem, load,
):
    t, p = lax.axis_index("tile"), lax.axis_index("plane")
    last = lax.axis_size("tile") - 1
    chip, core = p // 2, p % 2
    other = chip * 2 + 1 - core
    peers = [other] + [(chip + dz) % 4 * 2 + core for dz in range(1, 4)]
    sources = [other] + [(chip + 4 - dz) % 4 * 2 + core for dz in range(1, 4)]

    barrier = pltpu.get_barrier_semaphore()

    def greet(tile, plane):
        pl.semaphore_signal(barrier, inc=1, device_id=(tile, plane), device_id_type=MESH)

    @pl.when(t < last)
    def _():
        greet(t + 1, p)

    @pl.when(t > 0)
    def _():
        greet(t - 1, p)

    for dz in range(4):
        greet(t, peers[dz])

    loads = [
        pltpu.make_async_copy(src_hbm, src_raw, load.at[0]),
        pltpu.make_async_copy(ref_hbm, ref_raw, load.at[1]),
        pltpu.make_async_copy(sh_hbm, sh_ref, load.at[2]),
        pltpu.make_async_copy(w1_hbm, w_raw.at[0], load.at[3]),
        pltpu.make_async_copy(w2_hbm, w_raw.at[1], load.at[4]),
        pltpu.make_async_copy(place_hbm, place, load.at[5]),
        pltpu.make_async_copy(b1_hbm, small_out.at[0], load.at[6]),
        pltpu.make_async_copy(b2_hbm, small_out.at[1], load.at[7]),
        pltpu.make_async_copy(head_hbm, small_out.at[2], load.at[8]),
    ]
    for one in loads:
        one.start()
    for one in loads[:3]:
        one.wait()
    own = src_raw[...].reshape(64, 256)
    wide = ref_raw[...].reshape(128, 256)
    whole = jnp.concatenate([own[:, :128], jnp.zeros((64, 128), BF16)], axis=0)
    amounts = jnp.concatenate([sh_ref[...].astype(F32), jnp.zeros((4, 120), F32)], axis=1)
    amounts = jnp.concatenate([jnp.zeros((4, 128), F32), amounts], axis=0)
    head = pick(marks(8, ((0, 0), (1, 1))), whole) + pick(marks(8, ((2, 0), (3, 1))), wide[:, :128])
    tail = pick(marks(8, ((0, 126), (1, 127))), whole) + pick(marks(8, ((2, 126), (3, 127))), wide[:, 128:])
    pack_ref[0:64, :] = own
    pack_ref[64:72, 0:128] = (head + amounts).astype(BF16)
    pack_ref[64:72, 128:256] = tail.astype(BF16)
    wide_ref[:, 0:256] = wide

    sides = jnp.where(t < last, 1, 0) + jnp.where(t > 0, 1, 0)
    pl.semaphore_wait(barrier, 4 + sides)

    def copy(src, dst, from_sem, to_sem, tile, plane):
        return pltpu.make_async_remote_copy(
            src_ref=src, dst_ref=dst, send_sem=from_sem, recv_sem=to_sem,
            device_id=(tile, plane), device_id_type=MESH,
        )

    right = copy(pack_ref.at[:, 128:256], l_ref.at[p], send.at[0, 4], recv.at[0, 4], t + 1, p)
    left = copy(pack_ref.at[64:72, 0:128], r_ref.at[p], send.at[1, 4], recv.at[1, 4], t - 1, p)
    bufs = (g_ref, l_ref, r_ref)

    def spread(kind, dz):
        src = pack_ref if kind == 0 else bufs[kind].at[p]
        return copy(src, bufs[kind].at[p], send.at[kind, dz], recv.at[kind, dz], t, peers[dz])

    def passing(kind, dz):
        slot = bufs[kind].at[sources[dz]]
        return copy(slot, slot, pass_send.at[kind, dz], pass_recv.at[kind, dz], t, other)

    mine = pltpu.make_async_copy(pack_ref, g_ref.at[p], own_sem)

    @pl.when(t < last)
    def _():
        right.start()

    @pl.when(t > 0)
    def _():
        left.start()

    for dz in (2, 1, 3, 0):
        spread(0, dz).start()
    mine.start()

    for one in loads[3:]:
        one.wait()
    banded(w_raw.at[0], place, w1_out, 5)
    banded(w_raw.at[1], place, w2_out, 4)

    @pl.when(t > 0)
    def _():
        right.wait_recv()
        for dz in (2, 1, 3, 0):
            spread(1, dz).start()

    @pl.when(t < last)
    def _():
        left.wait_recv()
        for dz in (2, 1, 3, 0):
            spread(2, dz).start()

    def relay(kind):
        for dz in (1, 3, 2):
            spread(kind, dz).wait_recv()
            passing(kind, dz).start()

    def finish(kind):
        spread(kind, 0).wait_recv()
        for dz in range(4):
            spread(kind, dz).wait_send()
        for dz in (1, 3, 2):
            passing(kind, dz).wait()

    relay(0)

    @pl.when(t > 0)
    def _():
        relay(1)

    @pl.when(t < last)
    def _():
        relay(2)

    mine.wait()
    finish(0)

    @pl.when(t > 0)
    def _():
        finish(1)
        left.wait_send()

    @pl.when(t < last)
    def _():
        finish(2)
        right.wait_send()

    zero = jnp.zeros((8, 128), BF16)
    sh_out[...] = g_ref[:, 64:72, 0:128].reshape(64, 128).astype(F32).astype(jnp.int32)

    def edges(q):
        after = jnp.where(t < last, r_ref[q], zero)
        before = jnp.where(t > 0, l_ref[q, 64:72, :], zero)
        return jnp.concatenate([after, before], axis=0)

    mark = marks(16, ((0, 0), (1, 1), (8, 126), (9, 127)))
    for q in range(8):
        e_ref[q] = unpick(edges(q), mark)[:64].astype(BF16)
    mark = marks(16, ((2, 0), (3, 1), (10, 126), (11, 127)))
    wide_ref[:, 256:384] = unpick(edges(0), mark).astype(BF16)


def call_exchange(src, ref, shifts, w1, w2, b1, b2, head):
    vmem = pl.BlockSpec(memory_space=pltpu.VMEM)
    hbm = pl.BlockSpec(memory_space=pltpu.HBM)
    place = jnp.asarray(placing(), BF16)
    return pl.pallas_call(
        exchange,
        out_shape=[
            jax.ShapeDtypeStruct((3, 1, 8), F32),
            jax.ShapeDtypeStruct((64, 128), jnp.int32),
            jax.ShapeDtypeStruct((8, 72, 256), BF16),
            jax.ShapeDtypeStruct((8, 72, 128), BF16),
            jax.ShapeDtypeStruct((8, 64, 128), BF16),
            jax.ShapeDtypeStruct((128, 384), BF16),
            jax.ShapeDtypeStruct((160, 768), BF16),
            jax.ShapeDtypeStruct((128, 768), BF16),
        ],
        in_specs=[hbm] * 9,
        out_specs=[vmem] * 8,
        scratch_shapes=[
            pltpu.VMEM((4, 4, 4, 256), BF16),
            pltpu.VMEM((32, 4, 256), BF16),
            pltpu.VMEM((4, 8), jnp.int32),
            pltpu.VMEM((2, 27, 8, 8), BF16),
            pltpu.VMEM((1024, 384), BF16),
            pltpu.VMEM((72, 256), BF16),
            pltpu.VMEM((8, 8, 128), BF16),
            pltpu.SemaphoreType.DMA((3, 5)),
            pltpu.SemaphoreType.DMA((3, 5)),
            pltpu.SemaphoreType.DMA((3, 4)),
            pltpu.SemaphoreType.DMA((3, 4)),
            pltpu.SemaphoreType.DMA,
            pltpu.SemaphoreType.DMA((9,)),
        ],
        compiler_params=pltpu.CompilerParams(
            collective_id=0, has_side_effects=True, vmem_limit_bytes=60 * 1024 * 1024
        ),
        name="exchange",
    )(src, ref, shifts, w1, w2, b1, b2, head, place)


def per_device(ref_feat, src_feat, shifts, conv_one, bias_one, conv_two, bias_two, view_head):
    def kernel_of(w):
        return jnp.transpose(w, (2, 3, 4, 0, 1)).reshape(27, 8, 8)

    shared = call_exchange(
        src_feat, ref_feat, shifts, kernel_of(conv_one), kernel_of(conv_two),
        bias_one.reshape(1, 8), bias_two.reshape(1, 8), view_head.reshape(1, 8),
    )
    return call_compute("plane", "tile", *shared)


def solution(mesh):
    from jax.sharding import PartitionSpec as P
    placed = (
        P(None, None, "tile"), P(None, "plane", None, "tile"), P(None, "plane"),
        P(), P(), P(), P(), P(),
    )
    return jax.shard_map(
        per_device, mesh=mesh, in_specs=placed, out_specs=P(None, "plane", None, "tile"), check_vma=False,
    )
```

```python
import functools
import numpy as np
import jax
import jax.numpy as jnp
from jax import lax
from jax.experimental import pallas as pl
from jax.experimental.pallas import tpu as pltpu

VIEWS = 4
CONV_ONE = ((0, 3), (3, 3), (6, 2), (8, 2))
CONV_TWO = ((0, 3), (3, 3), (6, 2))
F32 = jnp.float32
BF16 = jnp.bfloat16


def placing():
    table = np.zeros((4, 256, 384), np.float32)
    for ho in range(4):
        for a in range(3):
            for b in range(3):
                hi = ho + b - 1
                if not 0 <= hi < 4:
                    continue
                for e in range(3):
                    for i in range(8):
                        table[ho, (a * 9 + b * 3 + e) * 8 + i, a * 96 + e * 32 + i * 4 + hi] = 1
    return table.reshape(1024, 384)


def banded(w_ref, place_ref, out_ref, steps):
    flat = jnp.concatenate([w_ref[tap].astype(F32) for tap in range(27)], axis=1)
    flat = jnp.concatenate([flat, jnp.zeros((8, 40), F32)], axis=1).astype(BF16)
    row = lax.broadcasted_iota(jnp.int32, (32, 8), 0)
    col = lax.broadcasted_iota(jnp.int32, (32, 8), 1)
    spread = (row // 4 == col).astype(F32).astype(BF16)
    wide = jnp.dot(spread, flat, preferred_element_type=F32)
    which = lax.broadcasted_iota(jnp.int32, (32, 256), 0) % 4
    wide = jnp.concatenate(
        [jnp.where(which == ho, wide, 0.0) for ho in range(4)], axis=1
    ).astype(BF16)
    base = jnp.dot(wide, place_ref[...], preferred_element_type=F32)
    base = jnp.concatenate([base, jnp.zeros((32, 128), F32)], axis=1)
    for do in range(steps):
        out_ref[do * 32 : do * 32 + 32, :] = pltpu.roll(base, 96 * do, 1).astype(BF16) if do else base.astype(BF16)


def per_row(ref, k):
    low = lax.broadcasted_iota(jnp.int32, (8, 128), 0) < 4
    return [jnp.where(low, ref[k, 0, 2 * q], ref[k, 0, 2 * q + 1]) for q in range(4)]


def compute(
    plane_axis, tile_axis, small, sh, g_ref, l_ref, e_ref, r_ref, w1, w2, o_ref,
    src2, rf, x2, f2, acc, tot,
):
    p = lax.axis_index(plane_axis)
    t = lax.axis_index(tile_axis)
    last_p = lax.axis_size(plane_axis) - 1
    last_t = lax.axis_size(tile_axis) - 1
    lane = lax.broadcasted_iota(jnp.int32, (8, 128), 1)
    lane32 = lax.broadcasted_iota(jnp.int32, (32, 128), 1)
    sub = lax.broadcasted_iota(jnp.int32, (8, 128), 0)
    low = sub < 4
    for k in range(3):
        rf[k] = r_ref[:, k * 128 : k * 128 + 128].astype(F32) * 0.25
    bias_one, bias_two, head = per_row(small, 0), per_row(small, 1), per_row(small, 2)
    edge_keep = jnp.where(
        jnp.logical_or(jnp.logical_and(lane == 0, t < last_t), jnp.logical_and(lane == 127, t > 0)), 1.0, 0.0
    )

    def neighbours(tiles, lanes):
        n = len(tiles)
        tiles = [a.astype(BF16) for a in tiles]
        right = [pltpu.roll(a, 1, 1) for a in tiles]
        left = [pltpu.roll(a, 127, 1) for a in tiles]
        return (
            [jnp.where(lanes == 0, right[(k - 1) % n], right[k]) for k in range(n)],
            tiles,
            [jnp.where(lanes == 127, left[(k + 1) % n], left[k]) for k in range(n)],
        )

    def one_view(v, xs, f):
        x, src = xs, src2
        own = pl.ds(pl.multiple_of(v * 16, 16), 16)
        src[0] = jnp.where(t > 0, l_ref[:, own, :].reshape(128, 128), jnp.zeros((128, 128), BF16))
        both = g_ref[:, own, :].reshape(128, 256)
        src[1] = both[:, :128]
        src[2] = both[:, 128:]
        src[3] = e_ref[:, own, :].reshape(128, 128)

        def one_plane(d):
            if d < 2:
                s = sh[jnp.maximum(p - 1, 0) * 8 + 4 + v, 6 + d]
            elif d > 9:
                s = sh[jnp.minimum(p + 1, last_p) * 8 + 4 + v, d - 10]
            else:
                s = sh[p * 8 + 4 + v, d - 2]
            before = lane32 < s
            outer = jnp.logical_xor(before, lane32 < 64)
            parts = [[], [], []]
            for q in range(4):
                rows = slice(32 * q, 32 * q + 32)
                r = [pltpu.roll(src[k, rows, :], s, 1) for k in range(4)]
                tiles = (
                    jnp.where(before, r[0], r[1]),
                    jnp.where(before, r[1], r[2]),
                    jnp.where(outer, r[3], jnp.where(lane32 < 64, r[2], r[0])),
                )
                for k in range(3):
                    prod = tiles[k].astype(F32) * rf[k, rows, :]
                    v0 = prod[0:8] + prod[8:16]
                    v1 = prod[16:24] + prod[24:32]
                    both = jnp.where(low, v0, v1) + pltpu.roll(jnp.where(low, v1, v0), 4, 0)
                    parts[k].append(both)
            tiles = [jnp.concatenate(parts[k], axis=0) for k in range(3)]
            if d < 2:
                tiles = [jnp.where(p > 0, a, 0.0) for a in tiles]
            if d > 9:
                tiles = [jnp.where(p < last_p, a, 0.0) for a in tiles]
            base = d * 96
            for e, moved in enumerate(neighbours(tiles, lane32)):
                for k in range(3):
                    x[base + e * 32 : base + e * 32 + 32, k * 128 : k * 128 + 128] = moved[k]

        for d in range(12):
            one_plane(d)

        for first, count in CONV_ONE:
            depth = (count + 2) * 96
            raw = jnp.dot(
                w1[: count * 32, :depth], x[first * 96 : first * 96 + depth, :],
                preferred_element_type=F32,
            )
            for i in range(count):
                d = first + i
                tiles = []
                for k in range(3):
                    cols = slice(k * 128, k * 128 + 128)
                    rows = []
                    for q in range(4):
                        at = i * 32 + q * 8
                        val = jnp.maximum(raw[at : at + 8, cols] + bias_one[q], 0.0)
                        if k == 2:
                            val = val * edge_keep
                        if d == 0:
                            val = jnp.where(p > 0, val, 0.0)
                        if d == 9:
                            val = jnp.where(p < last_p, val, 0.0)
                        rows.append(val)
                    tiles.append(jnp.concatenate(rows, axis=0))
                for e, moved in enumerate(neighbours(tiles, lane32)):
                    for k in range(2):
                        f[d * 96 + e * 32 : d * 96 + e * 32 + 32, k * 128 : k * 128 + 128] = moved[k]

        for first, count in CONV_TWO:
            depth = (count + 2) * 96
            raw = jnp.dot(
                w2[: count * 32, :depth], f[first * 96 : first * 96 + depth, :],
                preferred_element_type=F32,
            )
            for i in range(count):
                d = first + i
                for k in range(2):
                    cols = slice(k * 128, k * 128 + 128)
                    score = None
                    for q in range(4):
                        at = i * 32 + q * 8
                        term = jnp.maximum(raw[at : at + 8, cols] + bias_two[q], 0.0) * head[q]
                        score = term if score is None else score + term
                    score = score + pltpu.roll(score, 4, 0)
                    weight = 1.0 / (1.0 + jnp.exp(-score))
                    at = (d + 2) * 96 + 32
                    match = x[at : at + 32, cols].astype(F32)
                    tot[d, :, cols] = tot[d, :, cols] + weight
                    for q in range(4):
                        rows = slice(q * 8, q * 8 + 8)
                        acc[d, rows, cols] = acc[d, rows, cols] + weight * match[rows]

    def two_views(i, carry):
        one_view(i, x2.at[0], f2.at[0])
        return carry

    acc[...] = jnp.zeros_like(acc)
    tot[...] = jnp.zeros_like(tot)
    lax.fori_loop(0, VIEWS, two_views, 0)
    for d in range(8):
        for q in range(4):
            val = (acc[d, q * 8 : q * 8 + 8, :] / tot[d]).astype(BF16)
            o_ref[2 * q, d] = val[0:4]
            o_ref[2 * q + 1, d] = val[4:8]


def call_compute(plane_axis, tile_axis, small, sh, g, l, e, r, w1, w2):
    smem = pl.BlockSpec(memory_space=pltpu.SMEM)
    vmem = pl.BlockSpec(memory_space=pltpu.VMEM)
    return pl.pallas_call(
        functools.partial(compute, plane_axis, tile_axis),
        out_shape=jax.ShapeDtypeStruct((8, 8, 4, 256), BF16),
        in_specs=[smem, smem] + [vmem] * 6,
        out_specs=vmem,
        scratch_shapes=[
            pltpu.VMEM((4, 128, 128), BF16),
            pltpu.VMEM((3, 128, 128), F32),
            pltpu.VMEM((2, 1152, 384), BF16),
            pltpu.VMEM((2, 960, 256), BF16),
            pltpu.VMEM((8, 32, 256), F32),
            pltpu.VMEM((8, 8, 256), F32),
        ],
        compiler_params=pltpu.CompilerParams(vmem_limit_bytes=60 * 1024 * 1024),
        name="cost_volume",
    )(small, sh, g, l, e, r, w1, w2)


MESH = pl.DeviceIdType.MESH


def marks(rows, pairs):
    row = lax.broadcasted_iota(jnp.int32, (rows, 128), 0)
    lane = lax.broadcasted_iota(jnp.int32, (rows, 128), 1)
    hit = None
    for r, l in pairs:
        here = jnp.logical_and(row == r, lane == l)
        hit = here if hit is None else jnp.logical_or(hit, here)
    return jnp.where(hit, 1.0, 0.0).astype(BF16)


def pick(mark, rows):
    return lax.dot_general(mark, rows, (((1,), (1,)), ((), ())), preferred_element_type=F32)


def unpick(rows, mark):
    return lax.dot_general(rows, mark, (((0,), (0,)), ((), ())), preferred_element_type=F32)


def exchange(
    src_hbm, ref_hbm, sh_hbm, w1_hbm, w2_hbm, b1_hbm, b2_hbm, head_hbm, place_hbm, small_out, sh_out, g_ref, l_ref, e_ref, wide_ref, w1_out, w2_out,
    src_raw, ref_raw, sh_ref, w_raw, place, pack_ref, r_ref, send, recv, pass_send, pass_recv, own_sem, load,
):
    t, p = lax.axis_index("tile"), lax.axis_index("plane")
    last = lax.axis_size("tile") - 1
    chip, core = p // 2, p % 2
    other = chip * 2 + 1 - core
    peers = [other] + [(chip + dz) % 4 * 2 + core for dz in range(1, 4)]
    sources = [other] + [(chip + 4 - dz) % 4 * 2 + core for dz in range(1, 4)]

    barrier = pltpu.get_barrier_semaphore()

    def greet(tile, plane):
        pl.semaphore_signal(barrier, inc=1, device_id=(tile, plane), device_id_type=MESH)

    @pl.when(t < last)
    def _():
        greet(t + 1, p)

    @pl.when(t > 0)
    def _():
        greet(t - 1, p)

    for dz in range(4):
        greet(t, peers[dz])

    loads = [
        pltpu.make_async_copy(src_hbm, src_raw, load.at[0]),
        pltpu.make_async_copy(ref_hbm, ref_raw, load.at[1]),
        pltpu.make_async_copy(sh_hbm, sh_ref, load.at[2]),
        pltpu.make_async_copy(w1_hbm, w_raw.at[0], load.at[3]),
        pltpu.make_async_copy(w2_hbm, w_raw.at[1], load.at[4]),
        pltpu.make_async_copy(place_hbm, place, load.at[5]),
        pltpu.make_async_copy(b1_hbm, small_out.at[0], load.at[6]),
        pltpu.make_async_copy(b2_hbm, small_out.at[1], load.at[7]),
        pltpu.make_async_copy(head_hbm, small_out.at[2], load.at[8]),
    ]
    for one in loads:
        one.start()
    for one in loads[:3]:
        one.wait()
    own = src_raw[...].reshape(64, 256)
    wide = ref_raw[...].reshape(128, 256)
    whole = jnp.concatenate([own[:, :128], jnp.zeros((64, 128), BF16)], axis=0)
    amounts = jnp.concatenate([sh_ref[...].astype(F32), jnp.zeros((4, 120), F32)], axis=1)
    amounts = jnp.concatenate([jnp.zeros((4, 128), F32), amounts], axis=0)
    head = pick(marks(8, ((0, 0), (1, 1))), whole) + pick(marks(8, ((2, 0), (3, 1))), wide[:, :128])
    tail = pick(marks(8, ((0, 126), (1, 127))), whole) + pick(marks(8, ((2, 126), (3, 127))), wide[:, 128:])
    pack_ref[0:64, :] = own
    pack_ref[64:72, 0:128] = (head + amounts).astype(BF16)
    pack_ref[64:72, 128:256] = tail.astype(BF16)
    wide_ref[:, 0:256] = wide

    sides = jnp.where(t < last, 1, 0) + jnp.where(t > 0, 1, 0)
    pl.semaphore_wait(barrier, 4 + sides)

    def copy(src, dst, from_sem, to_sem, tile, plane):
        return pltpu.make_async_remote_copy(
            src_ref=src, dst_ref=dst, send_sem=from_sem, recv_sem=to_sem,
            device_id=(tile, plane), device_id_type=MESH,
        )

    right = copy(pack_ref.at[:, 128:256], l_ref.at[p], send.at[0, 4], recv.at[0, 4], t + 1, p)
    left = copy(pack_ref.at[64:72, 0:128], r_ref.at[p], send.at[1, 4], recv.at[1, 4], t - 1, p)
    bufs = (g_ref, l_ref, r_ref)

    def spread(kind, dz):
        src = pack_ref if kind == 0 else bufs[kind].at[p]
        return copy(src, bufs[kind].at[p], send.at[kind, dz], recv.at[kind, dz], t, peers[dz])

    def passing(kind, dz):
        slot = bufs[kind].at[sources[dz]]
        return copy(slot, slot, pass_send.at[kind, dz], pass_recv.at[kind, dz], t, other)

    mine = pltpu.make_async_copy(pack_ref, g_ref.at[p], own_sem)

    @pl.when(t < last)
    def _():
        right.start()

    @pl.when(t > 0)
    def _():
        left.start()

    for dz in (2, 1, 3, 0):
        spread(0, dz).start()
    mine.start()

    for one in loads[3:]:
        one.wait()
    banded(w_raw.at[0], place, w1_out, 3)
    banded(w_raw.at[1], place, w2_out, 3)

    @pl.when(t > 0)
    def _():
        right.wait_recv()
        for dz in (2, 1, 3, 0):
            spread(1, dz).start()

    @pl.when(t < last)
    def _():
        left.wait_recv()
        for dz in (2, 1, 3, 0):
            spread(2, dz).start()

    def relay(kind):
        for dz in (1, 3, 2):
            spread(kind, dz).wait_recv()
            passing(kind, dz).start()

    def finish(kind):
        spread(kind, 0).wait_recv()
        for dz in range(4):
            spread(kind, dz).wait_send()
        for dz in (1, 3, 2):
            passing(kind, dz).wait()

    relay(0)

    @pl.when(t > 0)
    def _():
        relay(1)

    @pl.when(t < last)
    def _():
        relay(2)

    mine.wait()
    finish(0)

    @pl.when(t > 0)
    def _():
        finish(1)
        left.wait_send()

    @pl.when(t < last)
    def _():
        finish(2)
        right.wait_send()

    zero = jnp.zeros((8, 128), BF16)
    sh_out[...] = g_ref[:, 64:72, 0:128].reshape(64, 128).astype(F32).astype(jnp.int32)

    def edges(q):
        after = jnp.where(t < last, r_ref[q], zero)
        before = jnp.where(t > 0, l_ref[q, 64:72, :], zero)
        return jnp.concatenate([after, before], axis=0)

    mark = marks(16, ((0, 0), (1, 1), (8, 126), (9, 127)))
    for q in range(8):
        e_ref[q] = unpick(edges(q), mark)[:64].astype(BF16)
    mark = marks(16, ((2, 0), (3, 1), (10, 126), (11, 127)))
    wide_ref[:, 256:384] = unpick(edges(0), mark).astype(BF16)


def call_exchange(src, ref, shifts, w1, w2, b1, b2, head):
    vmem = pl.BlockSpec(memory_space=pltpu.VMEM)
    hbm = pl.BlockSpec(memory_space=pltpu.HBM)
    place = jnp.asarray(placing(), BF16)
    return pl.pallas_call(
        exchange,
        out_shape=[
            jax.ShapeDtypeStruct((3, 1, 8), F32),
            jax.ShapeDtypeStruct((64, 128), jnp.int32),
            jax.ShapeDtypeStruct((8, 72, 256), BF16),
            jax.ShapeDtypeStruct((8, 72, 128), BF16),
            jax.ShapeDtypeStruct((8, 64, 128), BF16),
            jax.ShapeDtypeStruct((128, 384), BF16),
            jax.ShapeDtypeStruct((96, 512), BF16),
            jax.ShapeDtypeStruct((96, 512), BF16),
        ],
        in_specs=[hbm] * 9,
        out_specs=[vmem] * 8,
        scratch_shapes=[
            pltpu.VMEM((4, 4, 4, 256), BF16),
            pltpu.VMEM((32, 4, 256), BF16),
            pltpu.VMEM((4, 8), jnp.int32),
            pltpu.VMEM((2, 27, 8, 8), BF16),
            pltpu.VMEM((1024, 384), BF16),
            pltpu.VMEM((72, 256), BF16),
            pltpu.VMEM((8, 8, 128), BF16),
            pltpu.SemaphoreType.DMA((3, 5)),
            pltpu.SemaphoreType.DMA((3, 5)),
            pltpu.SemaphoreType.DMA((3, 4)),
            pltpu.SemaphoreType.DMA((3, 4)),
            pltpu.SemaphoreType.DMA,
            pltpu.SemaphoreType.DMA((9,)),
        ],
        compiler_params=pltpu.CompilerParams(
            collective_id=0, has_side_effects=True, vmem_limit_bytes=60 * 1024 * 1024
        ),
        name="exchange",
    )(src, ref, shifts, w1, w2, b1, b2, head, place)


def per_device(ref_feat, src_feat, shifts, conv_one, bias_one, conv_two, bias_two, view_head):
    def kernel_of(w):
        return jnp.transpose(w, (2, 3, 4, 0, 1)).reshape(27, 8, 8)

    shared = call_exchange(
        src_feat, ref_feat, shifts, kernel_of(conv_one), kernel_of(conv_two),
        bias_one.reshape(1, 8), bias_two.reshape(1, 8), view_head.reshape(1, 8),
    )
    return call_compute("plane", "tile", *shared)


def solution(mesh):
    from jax.sharding import PartitionSpec as P
    placed = (
        P(None, None, "tile"), P(None, "plane", None, "tile"), P(None, "plane"),
        P(), P(), P(), P(), P(),
    )
    return jax.shard_map(
        per_device, mesh=mesh, in_specs=placed, out_specs=P(None, "plane", None, "tile"), check_vma=False,
    )
```

```python
import functools
import numpy as np
import jax
import jax.numpy as jnp
from jax import lax
from jax.experimental import pallas as pl
from jax.experimental.pallas import tpu as pltpu

VIEWS = 4
CONV_ONE = ((0, 3), (3, 3), (6, 2), (8, 2))
CONV_TWO = ((0, 3), (3, 3), (6, 2))
F32 = jnp.float32
BF16 = jnp.bfloat16


def placing():
    table = np.zeros((4, 256, 384), np.float32)
    for ho in range(4):
        for a in range(3):
            for b in range(3):
                hi = ho + b - 1
                if not 0 <= hi < 4:
                    continue
                for e in range(3):
                    for i in range(8):
                        table[ho, (a * 9 + b * 3 + e) * 8 + i, a * 96 + e * 32 + i * 4 + hi] = 1
    return table.reshape(1024, 384)


def banded(w_ref, place_ref, out_ref, steps):
    flat = jnp.concatenate([w_ref[tap].astype(F32) for tap in range(27)], axis=1)
    flat = jnp.concatenate([flat, jnp.zeros((8, 40), F32)], axis=1).astype(BF16)
    row = lax.broadcasted_iota(jnp.int32, (32, 8), 0)
    col = lax.broadcasted_iota(jnp.int32, (32, 8), 1)
    spread = (row // 4 == col).astype(F32).astype(BF16)
    wide = jnp.dot(spread, flat, preferred_element_type=F32)
    which = lax.broadcasted_iota(jnp.int32, (32, 256), 0) % 4
    wide = jnp.concatenate(
        [jnp.where(which == ho, wide, 0.0) for ho in range(4)], axis=1
    ).astype(BF16)
    base = jnp.dot(wide, place_ref[...], preferred_element_type=F32)
    base = jnp.concatenate([base, jnp.zeros((32, 128), F32)], axis=1)
    for do in range(steps):
        out_ref[do * 32 : do * 32 + 32, :] = pltpu.roll(base, 96 * do, 1).astype(BF16) if do else base.astype(BF16)


def per_row(ref, k):
    low = lax.broadcasted_iota(jnp.int32, (8, 128), 0) < 4
    return [jnp.where(low, ref[k, 0, 2 * q], ref[k, 0, 2 * q + 1]) for q in range(4)]


def compute(
    plane_axis, tile_axis, small, sh, g_ref, l_ref, e_ref, r_ref, w1, w2, o_ref,
    src2, rf, x2, f2, acc, tot,
):
    p = lax.axis_index(plane_axis)
    t = lax.axis_index(tile_axis)
    last_p = lax.axis_size(plane_axis) - 1
    last_t = lax.axis_size(tile_axis) - 1
    lane = lax.broadcasted_iota(jnp.int32, (8, 128), 1)
    lane32 = lax.broadcasted_iota(jnp.int32, (32, 128), 1)
    sub = lax.broadcasted_iota(jnp.int32, (8, 128), 0)
    low = sub < 4
    for k in range(3):
        rf[k] = r_ref[:, k * 128 : k * 128 + 128].astype(F32) * 0.25
    bias_one, bias_two, head = per_row(small, 0), per_row(small, 1), per_row(small, 2)
    edge_keep = jnp.where(
        jnp.logical_or(jnp.logical_and(lane == 0, t < last_t), jnp.logical_and(lane == 127, t > 0)), 1.0, 0.0
    )

    def neighbours(tiles, lanes, keep):
        n = len(tiles)
        tiles = [a.astype(BF16) for a in tiles]
        return (
            [pltpu.roll(jnp.where(lanes == 127, tiles[k - 1], tiles[k]), 1, 1) for k in range(keep)],
            tiles,
            [pltpu.roll(jnp.where(lanes == 0, tiles[(k + 1) % n], tiles[k]), 127, 1) for k in range(keep)],
        )

    def one_view(v, xs, f):
        x, src = xs, src2
        own = pl.ds(pl.multiple_of(v * 16, 16), 16)
        src[0] = jnp.where(t > 0, l_ref[:, own, :].reshape(128, 128), jnp.zeros((128, 128), BF16))
        both = g_ref[:, own, :].reshape(128, 256)
        src[1] = both[:, :128]
        src[2] = both[:, 128:]
        src[3] = e_ref[:, own, :].reshape(128, 128)

        def one_plane(d):
            if d < 2:
                s = sh[jnp.maximum(p - 1, 0) * 8 + 4 + v, 6 + d]
            elif d > 9:
                s = sh[jnp.minimum(p + 1, last_p) * 8 + 4 + v, d - 10]
            else:
                s = sh[p * 8 + 4 + v, d - 2]
            lands = (lane32 + s) & 127
            before = lands < s
            first_half = lands < 64
            outer = jnp.logical_xor(before, first_half)
            parts = [[], [], []]
            for q in range(4):
                rows = slice(32 * q, 32 * q + 32)
                r = [src[k, rows, :] for k in range(4)]
                tiles = (
                    jnp.where(before, r[0], r[1]),
                    jnp.where(before, r[1], r[2]),
                    jnp.where(outer, r[3], jnp.where(first_half, r[2], r[0])),
                )
                tiles = [pltpu.roll(a, s, 1) for a in tiles]
                for k in range(3):
                    prod = tiles[k].astype(F32) * rf[k, rows, :]
                    v0 = prod[0:8] + prod[8:16]
                    v1 = prod[16:24] + prod[24:32]
                    both = jnp.where(low, v0, v1) + pltpu.roll(jnp.where(low, v1, v0), 4, 0)
                    parts[k].append(both)
            tiles = [jnp.concatenate(parts[k], axis=0) for k in range(3)]
            if d < 2:
                tiles = [jnp.where(p > 0, a, 0.0) for a in tiles]
            if d > 9:
                tiles = [jnp.where(p < last_p, a, 0.0) for a in tiles]
            base = d * 96
            for e, moved in enumerate(neighbours(tiles, lane32, 3)):
                for k in range(3):
                    x[base + e * 32 : base + e * 32 + 32, k * 128 : k * 128 + 128] = moved[k]

        for d in range(12):
            one_plane(d)

        for first, count in CONV_ONE:
            depth = (count + 2) * 96
            raw = jnp.dot(
                w1[: count * 32, :depth], x[first * 96 : first * 96 + depth, :],
                preferred_element_type=F32,
            )
            for i in range(count):
                d = first + i
                tiles = []
                for k in range(3):
                    cols = slice(k * 128, k * 128 + 128)
                    rows = []
                    for q in range(4):
                        at = i * 32 + q * 8
                        val = jnp.maximum(raw[at : at + 8, cols] + bias_one[q], 0.0)
                        if k == 2:
                            val = val * edge_keep
                        if d == 0:
                            val = jnp.where(p > 0, val, 0.0)
                        if d == 9:
                            val = jnp.where(p < last_p, val, 0.0)
                        rows.append(val)
                    tiles.append(jnp.concatenate(rows, axis=0))
                for e, moved in enumerate(neighbours(tiles, lane32, 2)):
                    for k in range(2):
                        f[d * 96 + e * 32 : d * 96 + e * 32 + 32, k * 128 : k * 128 + 128] = moved[k]

        for first, count in CONV_TWO:
            depth = (count + 2) * 96
            raw = jnp.dot(
                w2[: count * 32, :depth], f[first * 96 : first * 96 + depth, :],
                preferred_element_type=F32,
            )
            for i in range(count):
                d = first + i
                for k in range(2):
                    cols = slice(k * 128, k * 128 + 128)
                    score = None
                    for q in range(4):
                        at = i * 32 + q * 8
                        term = jnp.maximum(raw[at : at + 8, cols] + bias_two[q], 0.0) * head[q]
                        score = term if score is None else score + term
                    score = score + pltpu.roll(score, 4, 0)
                    weight = 1.0 / (1.0 + jnp.exp(-score))
                    at = (d + 2) * 96 + 32
                    match = x[at : at + 32, cols].astype(F32)
                    tot[d, :, cols] = tot[d, :, cols] + weight
                    for q in range(4):
                        rows = slice(q * 8, q * 8 + 8)
                        acc[d, rows, cols] = acc[d, rows, cols] + weight * match[rows]

    def two_views(i, carry):
        one_view(i, x2.at[0], f2.at[0])
        return carry

    acc[...] = jnp.zeros_like(acc)
    tot[...] = jnp.zeros_like(tot)
    lax.fori_loop(0, VIEWS, two_views, 0)
    for d in range(8):
        for q in range(4):
            val = (acc[d, q * 8 : q * 8 + 8, :] / tot[d]).astype(BF16)
            o_ref[2 * q, d] = val[0:4]
            o_ref[2 * q + 1, d] = val[4:8]


def call_compute(plane_axis, tile_axis, small, sh, g, l, e, r, w1, w2):
    smem = pl.BlockSpec(memory_space=pltpu.SMEM)
    vmem = pl.BlockSpec(memory_space=pltpu.VMEM)
    return pl.pallas_call(
        functools.partial(compute, plane_axis, tile_axis),
        out_shape=jax.ShapeDtypeStruct((8, 8, 4, 256), BF16),
        in_specs=[smem, smem] + [vmem] * 6,
        out_specs=vmem,
        scratch_shapes=[
            pltpu.VMEM((4, 128, 128), BF16),
            pltpu.VMEM((3, 128, 128), F32),
            pltpu.VMEM((2, 1152, 384), BF16),
            pltpu.VMEM((2, 960, 256), BF16),
            pltpu.VMEM((8, 32, 256), F32),
            pltpu.VMEM((8, 8, 256), F32),
        ],
        compiler_params=pltpu.CompilerParams(vmem_limit_bytes=60 * 1024 * 1024),
        name="cost_volume",
    )(small, sh, g, l, e, r, w1, w2)


MESH = pl.DeviceIdType.MESH


def marks(rows, pairs):
    row = lax.broadcasted_iota(jnp.int32, (rows, 128), 0)
    lane = lax.broadcasted_iota(jnp.int32, (rows, 128), 1)
    hit = None
    for r, l in pairs:
        here = jnp.logical_and(row == r, lane == l)
        hit = here if hit is None else jnp.logical_or(hit, here)
    return jnp.where(hit, 1.0, 0.0).astype(BF16)


def pick(mark, rows):
    return lax.dot_general(mark, rows, (((1,), (1,)), ((), ())), preferred_element_type=F32)


def unpick(rows, mark):
    return lax.dot_general(rows, mark, (((0,), (0,)), ((), ())), preferred_element_type=F32)


def exchange(
    src_hbm, ref_hbm, sh_hbm, w1_hbm, w2_hbm, b1_hbm, b2_hbm, head_hbm, place_hbm, small_out, sh_out, g_ref, l_ref, e_ref, wide_ref, w1_out, w2_out,
    src_raw, ref_raw, sh_ref, w_raw, place, pack_ref, r_ref, send, recv, pass_send, pass_recv, own_sem, load,
):
    t, p = lax.axis_index("tile"), lax.axis_index("plane")
    last = lax.axis_size("tile") - 1
    chip, core = p // 2, p % 2
    other = chip * 2 + 1 - core
    peers = [other] + [(chip + dz) % 4 * 2 + core for dz in range(1, 4)]
    sources = [other] + [(chip + 4 - dz) % 4 * 2 + core for dz in range(1, 4)]

    barrier = pltpu.get_barrier_semaphore()

    def greet(tile, plane):
        pl.semaphore_signal(barrier, inc=1, device_id=(tile, plane), device_id_type=MESH)

    @pl.when(t < last)
    def _():
        greet(t + 1, p)

    @pl.when(t > 0)
    def _():
        greet(t - 1, p)

    for dz in range(4):
        greet(t, peers[dz])

    loads = [
        pltpu.make_async_copy(src_hbm, src_raw, load.at[0]),
        pltpu.make_async_copy(ref_hbm, ref_raw, load.at[1]),
        pltpu.make_async_copy(sh_hbm, sh_ref, load.at[2]),
        pltpu.make_async_copy(w1_hbm, w_raw.at[0], load.at[3]),
        pltpu.make_async_copy(w2_hbm, w_raw.at[1], load.at[4]),
        pltpu.make_async_copy(place_hbm, place, load.at[5]),
        pltpu.make_async_copy(b1_hbm, small_out.at[0], load.at[6]),
        pltpu.make_async_copy(b2_hbm, small_out.at[1], load.at[7]),
        pltpu.make_async_copy(head_hbm, small_out.at[2], load.at[8]),
    ]
    for one in loads:
        one.start()
    for one in loads[:3]:
        one.wait()
    own = src_raw[...].reshape(64, 256)
    wide = ref_raw[...].reshape(128, 256)
    whole = jnp.concatenate([own[:, :128], jnp.zeros((64, 128), BF16)], axis=0)
    amounts = jnp.concatenate([sh_ref[...].astype(F32), jnp.zeros((4, 120), F32)], axis=1)
    amounts = jnp.concatenate([jnp.zeros((4, 128), F32), amounts], axis=0)
    head = pick(marks(8, ((0, 0), (1, 1))), whole) + pick(marks(8, ((2, 0), (3, 1))), wide[:, :128])
    tail = pick(marks(8, ((0, 126), (1, 127))), whole) + pick(marks(8, ((2, 126), (3, 127))), wide[:, 128:])
    pack_ref[0:64, :] = own
    pack_ref[64:72, 0:128] = (head + amounts).astype(BF16)
    pack_ref[64:72, 128:256] = tail.astype(BF16)
    wide_ref[:, 0:256] = wide

    sides = jnp.where(t < last, 1, 0) + jnp.where(t > 0, 1, 0)
    pl.semaphore_wait(barrier, 4 + sides)

    def copy(src, dst, from_sem, to_sem, tile, plane):
        return pltpu.make_async_remote_copy(
            src_ref=src, dst_ref=dst, send_sem=from_sem, recv_sem=to_sem,
            device_id=(tile, plane), device_id_type=MESH,
        )

    right = copy(pack_ref.at[:, 128:256], l_ref.at[p], send.at[0, 4], recv.at[0, 4], t + 1, p)
    left = copy(pack_ref.at[64:72, 0:128], r_ref.at[p], send.at[1, 4], recv.at[1, 4], t - 1, p)
    bufs = (g_ref, l_ref, r_ref)

    def spread(kind, dz):
        src = pack_ref if kind == 0 else bufs[kind].at[p]
        return copy(src, bufs[kind].at[p], send.at[kind, dz], recv.at[kind, dz], t, peers[dz])

    def passing(kind, dz):
        slot = bufs[kind].at[sources[dz]]
        return copy(slot, slot, pass_send.at[kind, dz], pass_recv.at[kind, dz], t, other)

    mine = pltpu.make_async_copy(pack_ref, g_ref.at[p], own_sem)

    @pl.when(t < last)
    def _():
        right.start()

    @pl.when(t > 0)
    def _():
        left.start()

    for dz in (2, 1, 3, 0):
        spread(0, dz).start()
    mine.start()

    for one in loads[3:]:
        one.wait()
    banded(w_raw.at[0], place, w1_out, 3)
    banded(w_raw.at[1], place, w2_out, 3)

    @pl.when(t > 0)
    def _():
        right.wait_recv()
        for dz in (2, 1, 3, 0):
            spread(1, dz).start()

    @pl.when(t < last)
    def _():
        left.wait_recv()
        for dz in (2, 1, 3, 0):
            spread(2, dz).start()

    def relay(kind):
        for dz in (1, 3, 2):
            spread(kind, dz).wait_recv()
            passing(kind, dz).start()

    def finish(kind):
        spread(kind, 0).wait_recv()
        for dz in range(4):
            spread(kind, dz).wait_send()
        for dz in (1, 3, 2):
            passing(kind, dz).wait()

    relay(0)

    @pl.when(t > 0)
    def _():
        relay(1)

    @pl.when(t < last)
    def _():
        relay(2)

    mine.wait()
    finish(0)

    @pl.when(t > 0)
    def _():
        finish(1)
        left.wait_send()

    @pl.when(t < last)
    def _():
        finish(2)
        right.wait_send()

    zero = jnp.zeros((8, 128), BF16)
    sh_out[...] = g_ref[:, 64:72, 0:128].reshape(64, 128).astype(F32).astype(jnp.int32)

    def edges(q):
        after = jnp.where(t < last, r_ref[q], zero)
        before = jnp.where(t > 0, l_ref[q, 64:72, :], zero)
        return jnp.concatenate([after, before], axis=0)

    mark = marks(16, ((0, 0), (1, 1), (8, 126), (9, 127)))
    for q in range(8):
        e_ref[q] = unpick(edges(q), mark)[:64].astype(BF16)
    mark = marks(16, ((2, 0), (3, 1), (10, 126), (11, 127)))
    wide_ref[:, 256:384] = unpick(edges(0), mark).astype(BF16)


def call_exchange(src, ref, shifts, w1, w2, b1, b2, head):
    vmem = pl.BlockSpec(memory_space=pltpu.VMEM)
    hbm = pl.BlockSpec(memory_space=pltpu.HBM)
    place = jnp.asarray(placing(), BF16)
    return pl.pallas_call(
        exchange,
        out_shape=[
            jax.ShapeDtypeStruct((3, 1, 8), F32),
            jax.ShapeDtypeStruct((64, 128), jnp.int32),
            jax.ShapeDtypeStruct((8, 72, 256), BF16),
            jax.ShapeDtypeStruct((8, 72, 128), BF16),
            jax.ShapeDtypeStruct((8, 64, 128), BF16),
            jax.ShapeDtypeStruct((128, 384), BF16),
            jax.ShapeDtypeStruct((96, 512), BF16),
            jax.ShapeDtypeStruct((96, 512), BF16),
        ],
        in_specs=[hbm] * 9,
        out_specs=[vmem] * 8,
        scratch_shapes=[
            pltpu.VMEM((4, 4, 4, 256), BF16),
            pltpu.VMEM((32, 4, 256), BF16),
            pltpu.VMEM((4, 8), jnp.int32),
            pltpu.VMEM((2, 27, 8, 8), BF16),
            pltpu.VMEM((1024, 384), BF16),
            pltpu.VMEM((72, 256), BF16),
            pltpu.VMEM((8, 8, 128), BF16),
            pltpu.SemaphoreType.DMA((3, 5)),
            pltpu.SemaphoreType.DMA((3, 5)),
            pltpu.SemaphoreType.DMA((3, 4)),
            pltpu.SemaphoreType.DMA((3, 4)),
            pltpu.SemaphoreType.DMA,
            pltpu.SemaphoreType.DMA((9,)),
        ],
        compiler_params=pltpu.CompilerParams(
            collective_id=0, has_side_effects=True, vmem_limit_bytes=60 * 1024 * 1024
        ),
        name="exchange",
    )(src, ref, shifts, w1, w2, b1, b2, head, place)


def per_device(ref_feat, src_feat, shifts, conv_one, bias_one, conv_two, bias_two, view_head):
    def kernel_of(w):
        return jnp.transpose(w, (2, 3, 4, 0, 1)).reshape(27, 8, 8)

    shared = call_exchange(
        src_feat, ref_feat, shifts, kernel_of(conv_one), kernel_of(conv_two),
        bias_one.reshape(1, 8), bias_two.reshape(1, 8), view_head.reshape(1, 8),
    )
    return call_compute("plane", "tile", *shared)


def solution(mesh):
    from jax.sharding import PartitionSpec as P
    placed = (
        P(None, None, "tile"), P(None, "plane", None, "tile"), P(None, "plane"),
        P(), P(), P(), P(), P(),
    )
    return jax.shard_map(
        per_device, mesh=mesh, in_specs=placed, out_specs=P(None, "plane", None, "tile"), check_vma=False,
    )
```

```python
import functools
import numpy as np
import jax
import jax.numpy as jnp
from jax import lax
from jax.experimental import pallas as pl
from jax.experimental.pallas import tpu as pltpu

VIEWS = 4
CONV_ONE = ((0, 3), (3, 3), (6, 2), (8, 2))
CONV_TWO = ((0, 2), (2, 2), (4, 2), (6, 2))
F32 = jnp.float32
BF16 = jnp.bfloat16


def placing():
    table = np.zeros((4, 256, 384), np.float32)
    for ho in range(4):
        for a in range(3):
            for b in range(3):
                hi = ho + b - 1
                if not 0 <= hi < 4:
                    continue
                for e in range(3):
                    for i in range(8):
                        table[ho, (a * 9 + b * 3 + e) * 8 + i, a * 96 + e * 32 + i * 4 + hi] = 1
    return table.reshape(1024, 384)


def banded(w_ref, place_ref, out_ref, steps):
    flat = jnp.concatenate([w_ref[tap].astype(F32) for tap in range(27)], axis=1)
    flat = jnp.concatenate([flat, jnp.zeros((8, 40), F32)], axis=1).astype(BF16)
    row = lax.broadcasted_iota(jnp.int32, (32, 8), 0)
    col = lax.broadcasted_iota(jnp.int32, (32, 8), 1)
    spread = (row // 4 == col).astype(F32).astype(BF16)
    wide = jnp.dot(spread, flat, preferred_element_type=F32)
    which = lax.broadcasted_iota(jnp.int32, (32, 256), 0) % 4
    wide = jnp.concatenate(
        [jnp.where(which == ho, wide, 0.0) for ho in range(4)], axis=1
    ).astype(BF16)
    base = jnp.dot(wide, place_ref[...], preferred_element_type=F32)
    base = jnp.concatenate([base, jnp.zeros((32, 128), F32)], axis=1)
    for do in range(steps):
        out_ref[do * 32 : do * 32 + 32, :] = pltpu.roll(base, 96 * do, 1).astype(BF16) if do else base.astype(BF16)


def per_row(ref, k):
    low = lax.broadcasted_iota(jnp.int32, (8, 128), 0) < 4
    return [jnp.where(low, ref[k, 0, 2 * q], ref[k, 0, 2 * q + 1]) for q in range(4)]


def compute(
    plane_axis, tile_axis, small, sh, g_ref, l_ref, e_ref, r_ref, w1, w2, o_ref,
    src2, rf, x2, f2, acc, tot,
):
    p = lax.axis_index(plane_axis)
    t = lax.axis_index(tile_axis)
    last_p = lax.axis_size(plane_axis) - 1
    last_t = lax.axis_size(tile_axis) - 1
    lane = lax.broadcasted_iota(jnp.int32, (8, 128), 1)
    lane32 = lax.broadcasted_iota(jnp.int32, (32, 128), 1)
    sub = lax.broadcasted_iota(jnp.int32, (8, 128), 0)
    low = sub < 4
    for k in range(3):
        rf[k] = r_ref[:, k * 128 : k * 128 + 128].astype(F32) * 0.25
    bias_one, bias_two, head = per_row(small, 0), per_row(small, 1), per_row(small, 2)
    edge_keep = jnp.where(
        jnp.logical_or(jnp.logical_and(lane == 0, t < last_t), jnp.logical_and(lane == 127, t > 0)), 1.0, 0.0
    )

    def neighbours(tiles, lanes, keep):
        n = len(tiles)
        tiles = [a.astype(BF16) for a in tiles]
        return (
            [pltpu.roll(jnp.where(lanes == 127, tiles[k - 1], tiles[k]), 1, 1) for k in range(keep)],
            tiles,
            [pltpu.roll(jnp.where(lanes == 0, tiles[(k + 1) % n], tiles[k]), 127, 1) for k in range(keep)],
        )

    def one_view(v, xs, f):
        x, src = xs, src2
        own = pl.ds(pl.multiple_of(v * 16, 16), 16)
        src[0] = jnp.where(t > 0, l_ref[:, own, :].reshape(128, 128), jnp.zeros((128, 128), BF16))
        both = g_ref[:, own, :].reshape(128, 256)
        src[1] = both[:, :128]
        src[2] = both[:, 128:]
        src[3] = e_ref[:, own, :].reshape(128, 128)

        def one_plane(d):
            if d < 2:
                s = sh[jnp.maximum(p - 1, 0) * 8 + 4 + v, 6 + d]
            elif d > 9:
                s = sh[jnp.minimum(p + 1, last_p) * 8 + 4 + v, d - 10]
            else:
                s = sh[p * 8 + 4 + v, d - 2]
            lands = (lane32 + s) & 127
            before = lands < s
            first_half = lands < 64
            outer = jnp.logical_xor(before, first_half)
            parts = [[], [], []]
            for q in range(4):
                rows = slice(32 * q, 32 * q + 32)
                r = [src[k, rows, :] for k in range(4)]
                tiles = (
                    jnp.where(before, r[0], r[1]),
                    jnp.where(before, r[1], r[2]),
                    jnp.where(outer, r[3], jnp.where(first_half, r[2], r[0])),
                )
                tiles = [pltpu.roll(a, s, 1) for a in tiles]
                for k in range(3):
                    prod = tiles[k].astype(F32) * rf[k, rows, :]
                    v0 = prod[0:8] + prod[8:16]
                    v1 = prod[16:24] + prod[24:32]
                    both = jnp.where(low, v0, v1) + pltpu.roll(jnp.where(low, v1, v0), 4, 0)
                    parts[k].append(both)
            tiles = [jnp.concatenate(parts[k], axis=0) for k in range(3)]
            if d < 2:
                tiles = [jnp.where(p > 0, a, 0.0) for a in tiles]
            if d > 9:
                tiles = [jnp.where(p < last_p, a, 0.0) for a in tiles]
            base = d * 96
            for e, moved in enumerate(neighbours(tiles, lane32, 3)):
                for k in range(3):
                    x[base + e * 32 : base + e * 32 + 32, k * 128 : k * 128 + 128] = moved[k]

        for d in range(12):
            one_plane(d)

        for first, count in CONV_ONE:
            depth = (count + 2) * 96
            raw = jnp.dot(
                w1[: count * 32, :depth], x[first * 96 : first * 96 + depth, :],
                preferred_element_type=F32,
            )
            for i in range(count):
                d = first + i
                tiles = []
                for k in range(3):
                    cols = slice(k * 128, k * 128 + 128)
                    rows = []
                    for q in range(4):
                        at = i * 32 + q * 8
                        val = jnp.maximum(raw[at : at + 8, cols] + bias_one[q], 0.0)
                        if k == 2:
                            val = val * edge_keep
                        if d == 0:
                            val = jnp.where(p > 0, val, 0.0)
                        if d == 9:
                            val = jnp.where(p < last_p, val, 0.0)
                        rows.append(val)
                    tiles.append(jnp.concatenate(rows, axis=0))
                for e, moved in enumerate(neighbours(tiles, lane32, 2)):
                    for k in range(2):
                        f[d * 96 + e * 32 : d * 96 + e * 32 + 32, k * 128 : k * 128 + 128] = moved[k]

        for first, count in CONV_TWO:
            depth = (count + 2) * 96
            raw = jnp.dot(
                w2[: count * 32, :depth], f[first * 96 : first * 96 + depth, :],
                preferred_element_type=F32,
            )
            for i in range(count):
                d = first + i
                for k in range(2):
                    cols = slice(k * 128, k * 128 + 128)
                    score = None
                    for q in range(4):
                        at = i * 32 + q * 8
                        term = jnp.maximum(raw[at : at + 8, cols] + bias_two[q], 0.0) * head[q]
                        score = term if score is None else score + term
                    score = score + pltpu.roll(score, 4, 0)
                    weight = 1.0 / (1.0 + jnp.exp(-score))
                    at = (d + 2) * 96 + 32
                    match = x[at : at + 32, cols].astype(F32)
                    tot[d, :, cols] = tot[d, :, cols] + weight
                    for q in range(4):
                        rows = slice(q * 8, q * 8 + 8)
                        acc[d, rows, cols] = acc[d, rows, cols] + weight * match[rows]

    def two_views(i, carry):
        one_view(i, x2.at[0], f2.at[0])
        return carry

    acc[...] = jnp.zeros_like(acc)
    tot[...] = jnp.zeros_like(tot)
    lax.fori_loop(0, VIEWS, two_views, 0)
    for d in range(8):
        for q in range(4):
            val = (acc[d, q * 8 : q * 8 + 8, :] / tot[d]).astype(BF16)
            o_ref[2 * q, d] = val[0:4]
            o_ref[2 * q + 1, d] = val[4:8]


def call_compute(plane_axis, tile_axis, small, sh, g, l, e, r, w1, w2):
    smem = pl.BlockSpec(memory_space=pltpu.SMEM)
    vmem = pl.BlockSpec(memory_space=pltpu.VMEM)
    return pl.pallas_call(
        functools.partial(compute, plane_axis, tile_axis),
        out_shape=jax.ShapeDtypeStruct((8, 8, 4, 256), BF16),
        in_specs=[smem, smem] + [vmem] * 6,
        out_specs=vmem,
        scratch_shapes=[
            pltpu.VMEM((4, 128, 128), BF16),
            pltpu.VMEM((3, 128, 128), F32),
            pltpu.VMEM((2, 1152, 384), BF16),
            pltpu.VMEM((2, 960, 256), BF16),
            pltpu.VMEM((8, 32, 256), F32),
            pltpu.VMEM((8, 8, 256), F32),
        ],
        compiler_params=pltpu.CompilerParams(vmem_limit_bytes=60 * 1024 * 1024),
        name="cost_volume",
    )(small, sh, g, l, e, r, w1, w2)


MESH = pl.DeviceIdType.MESH


def marks(rows, pairs):
    row = lax.broadcasted_iota(jnp.int32, (rows, 128), 0)
    lane = lax.broadcasted_iota(jnp.int32, (rows, 128), 1)
    hit = None
    for r, l in pairs:
        here = jnp.logical_and(row == r, lane == l)
        hit = here if hit is None else jnp.logical_or(hit, here)
    return jnp.where(hit, 1.0, 0.0).astype(BF16)


def pick(mark, rows):
    return lax.dot_general(mark, rows, (((1,), (1,)), ((), ())), preferred_element_type=F32)


def unpick(rows, mark):
    return lax.dot_general(rows, mark, (((0,), (0,)), ((), ())), preferred_element_type=F32)


def exchange(
    src_hbm, ref_hbm, sh_hbm, w1_hbm, w2_hbm, b1_hbm, b2_hbm, head_hbm, place_hbm, small_out, sh_out, g_ref, l_ref, e_ref, wide_ref, w1_out, w2_out,
    src_raw, ref_raw, sh_ref, w_raw, place, pack_ref, r_ref, send, recv, pass_send, pass_recv, own_sem, load,
):
    t, p = lax.axis_index("tile"), lax.axis_index("plane")
    last = lax.axis_size("tile") - 1
    chip, core = p // 2, p % 2
    other = chip * 2 + 1 - core
    peers = [other] + [(chip + dz) % 4 * 2 + core for dz in range(1, 4)]
    sources = [other] + [(chip + 4 - dz) % 4 * 2 + core for dz in range(1, 4)]

    barrier = pltpu.get_barrier_semaphore()

    def greet(tile, plane):
        pl.semaphore_signal(barrier, inc=1, device_id=(tile, plane), device_id_type=MESH)

    @pl.when(t < last)
    def _():
        greet(t + 1, p)

    @pl.when(t > 0)
    def _():
        greet(t - 1, p)

    for dz in range(4):
        greet(t, peers[dz])

    loads = [
        pltpu.make_async_copy(src_hbm, src_raw, load.at[0]),
        pltpu.make_async_copy(ref_hbm, ref_raw, load.at[1]),
        pltpu.make_async_copy(sh_hbm, sh_ref, load.at[2]),
        pltpu.make_async_copy(w1_hbm, w_raw.at[0], load.at[3]),
        pltpu.make_async_copy(w2_hbm, w_raw.at[1], load.at[4]),
        pltpu.make_async_copy(place_hbm, place, load.at[5]),
        pltpu.make_async_copy(b1_hbm, small_out.at[0], load.at[6]),
        pltpu.make_async_copy(b2_hbm, small_out.at[1], load.at[7]),
        pltpu.make_async_copy(head_hbm, small_out.at[2], load.at[8]),
    ]
    for one in loads:
        one.start()
    for one in loads[:3]:
        one.wait()
    own = src_raw[...].reshape(64, 256)
    wide = ref_raw[...].reshape(128, 256)
    whole = jnp.concatenate([own[:, :128], jnp.zeros((64, 128), BF16)], axis=0)
    amounts = jnp.concatenate([sh_ref[...].astype(F32), jnp.zeros((4, 120), F32)], axis=1)
    amounts = jnp.concatenate([jnp.zeros((4, 128), F32), amounts], axis=0)
    head = pick(marks(8, ((0, 0), (1, 1))), whole) + pick(marks(8, ((2, 0), (3, 1))), wide[:, :128])
    tail = pick(marks(8, ((0, 126), (1, 127))), whole) + pick(marks(8, ((2, 126), (3, 127))), wide[:, 128:])
    pack_ref[0:64, :] = own
    pack_ref[64:72, 0:128] = (head + amounts).astype(BF16)
    pack_ref[64:72, 128:256] = tail.astype(BF16)
    wide_ref[:, 0:256] = wide

    sides = jnp.where(t < last, 1, 0) + jnp.where(t > 0, 1, 0)
    pl.semaphore_wait(barrier, 4 + sides)

    def copy(src, dst, from_sem, to_sem, tile, plane):
        return pltpu.make_async_remote_copy(
            src_ref=src, dst_ref=dst, send_sem=from_sem, recv_sem=to_sem,
            device_id=(tile, plane), device_id_type=MESH,
        )

    right = copy(pack_ref.at[:, 128:256], l_ref.at[p], send.at[0, 4], recv.at[0, 4], t + 1, p)
    left = copy(pack_ref.at[64:72, 0:128], r_ref.at[p], send.at[1, 4], recv.at[1, 4], t - 1, p)
    bufs = (g_ref, l_ref, r_ref)

    def spread(kind, dz):
        src = pack_ref if kind == 0 else bufs[kind].at[p]
        return copy(src, bufs[kind].at[p], send.at[kind, dz], recv.at[kind, dz], t, peers[dz])

    def passing(kind, dz):
        slot = bufs[kind].at[sources[dz]]
        return copy(slot, slot, pass_send.at[kind, dz], pass_recv.at[kind, dz], t, other)

    mine = pltpu.make_async_copy(pack_ref, g_ref.at[p], own_sem)

    @pl.when(t < last)
    def _():
        right.start()

    @pl.when(t > 0)
    def _():
        left.start()

    for dz in (2, 1, 3, 0):
        spread(0, dz).start()
    mine.start()

    for one in loads[3:]:
        one.wait()
    banded(w_raw.at[0], place, w1_out, 3)
    banded(w_raw.at[1], place, w2_out, 3)

    def relay(kind):
        for dz in (1, 3, 2):
            spread(kind, dz).wait_recv()
            passing(kind, dz).start()

    def finish(kind):
        spread(kind, 0).wait_recv()
        for dz in range(4):
            spread(kind, dz).wait_send()
        for dz in (1, 3, 2):
            passing(kind, dz).wait()

    near_left, near_right = lax.rem(t, 16) != 0, lax.rem(t + 1, 16) != 0

    def onward(kind, arrival):
        arrival.wait_recv()
        for dz in (2, 1, 3, 0):
            spread(kind, dz).start()

    from_left, from_right = t > 0, t < last

    @pl.when(jnp.logical_and(from_left, near_left))
    def _():
        onward(1, right)

    @pl.when(jnp.logical_and(from_right, near_right))
    def _():
        onward(2, left)

    relay(0)

    @pl.when(jnp.logical_and(from_left, near_left))
    def _():
        relay(1)

    @pl.when(jnp.logical_and(from_right, near_right))
    def _():
        relay(2)

    @pl.when(jnp.logical_and(from_left, jnp.logical_not(near_left)))
    def _():
        onward(1, right)
        relay(1)

    @pl.when(jnp.logical_and(from_right, jnp.logical_not(near_right)))
    def _():
        onward(2, left)
        relay(2)

    mine.wait()
    finish(0)

    @pl.when(t > 0)
    def _():
        finish(1)
        left.wait_send()

    @pl.when(t < last)
    def _():
        finish(2)
        right.wait_send()

    zero = jnp.zeros((8, 128), BF16)
    sh_out[...] = g_ref[:, 64:72, 0:128].reshape(64, 128).astype(F32).astype(jnp.int32)

    def edges(q):
        after = jnp.where(t < last, r_ref[q], zero)
        before = jnp.where(t > 0, l_ref[q, 64:72, :], zero)
        return jnp.concatenate([after, before], axis=0)

    mark = marks(16, ((0, 0), (1, 1), (8, 126), (9, 127)))
    for q in range(8):
        e_ref[q] = unpick(edges(q), mark)[:64].astype(BF16)
    mark = marks(16, ((2, 0), (3, 1), (10, 126), (11, 127)))
    wide_ref[:, 256:384] = unpick(edges(0), mark).astype(BF16)


def call_exchange(src, ref, shifts, w1, w2, b1, b2, head):
    vmem = pl.BlockSpec(memory_space=pltpu.VMEM)
    hbm = pl.BlockSpec(memory_space=pltpu.HBM)
    place = jnp.asarray(placing(), BF16)
    return pl.pallas_call(
        exchange,
        out_shape=[
            jax.ShapeDtypeStruct((3, 1, 8), F32),
            jax.ShapeDtypeStruct((64, 128), jnp.int32),
            jax.ShapeDtypeStruct((8, 72, 256), BF16),
            jax.ShapeDtypeStruct((8, 72, 128), BF16),
            jax.ShapeDtypeStruct((8, 64, 128), BF16),
            jax.ShapeDtypeStruct((128, 384), BF16),
            jax.ShapeDtypeStruct((96, 512), BF16),
            jax.ShapeDtypeStruct((96, 512), BF16),
        ],
        in_specs=[hbm] * 9,
        out_specs=[vmem] * 8,
        scratch_shapes=[
            pltpu.VMEM((4, 4, 4, 256), BF16),
            pltpu.VMEM((32, 4, 256), BF16),
            pltpu.VMEM((4, 8), jnp.int32),
            pltpu.VMEM((2, 27, 8, 8), BF16),
            pltpu.VMEM((1024, 384), BF16),
            pltpu.VMEM((72, 256), BF16),
            pltpu.VMEM((8, 8, 128), BF16),
            pltpu.SemaphoreType.DMA((3, 5)),
            pltpu.SemaphoreType.DMA((3, 5)),
            pltpu.SemaphoreType.DMA((3, 4)),
            pltpu.SemaphoreType.DMA((3, 4)),
            pltpu.SemaphoreType.DMA,
            pltpu.SemaphoreType.DMA((9,)),
        ],
        compiler_params=pltpu.CompilerParams(
            collective_id=0, has_side_effects=True, vmem_limit_bytes=60 * 1024 * 1024
        ),
        name="exchange",
    )(src, ref, shifts, w1, w2, b1, b2, head, place)


def per_device(ref_feat, src_feat, shifts, conv_one, bias_one, conv_two, bias_two, view_head):
    def kernel_of(w):
        return jnp.transpose(w, (2, 3, 4, 0, 1)).reshape(27, 8, 8)

    shared = call_exchange(
        src_feat, ref_feat, shifts, kernel_of(conv_one), kernel_of(conv_two),
        bias_one.reshape(1, 8), bias_two.reshape(1, 8), view_head.reshape(1, 8),
    )
    return call_compute("plane", "tile", *shared)


def solution(mesh):
    from jax.sharding import PartitionSpec as P
    placed = (
        P(None, None, "tile"), P(None, "plane", None, "tile"), P(None, "plane"),
        P(), P(), P(), P(), P(),
    )
    return jax.shard_map(
        per_device, mesh=mesh, in_specs=placed, out_specs=P(None, "plane", None, "tile"), check_vma=False,
    )
```
